32 devices in a mesh: grp: 4 (over x, core), tp: 4 (over z), cores: 2 (over y).
Axes of the slice: x: 2, y: 2, z: 4, core: 2. Of those that a mesh axis runs over, the one named last changes fastest.
Arguments:
- tokens: bfloat16 [4096, 8192], P('grp', ('tp', 'cores')), may hold values from -6 to 6
- gate_up_weight: bfloat16 [8192, 2, 16384], P(None, None, ('tp', 'cores')), may hold values from -0.0625 to 0.0625
- down_factor_pool: bfloat16 [8, 8192, 256], P(('tp', 'cores'), 'grp'), may hold values from -0.0625 to 0.0625
- up_factor_pool: bfloat16 [8, 4, 8, 128, 1024], P(('tp', 'cores'), 'grp'), may hold values from -0.5 to 0.5
- segment_adapters: int32 [4, 3], replicated, may hold values from 0 to 7
- segment_tile_counts: int32 [4, 3], P('grp'), may hold values from 1 to 4, 8 in all within a row
- adapter_pool_rows: int32 [8], replicated, may hold values from 0 to 7, each once
Outputs:
- hidden: bfloat16 [4096, 16384], P('grp', ('tp', 'cores'))
The draws below stay inside these ranges and needn't reach their ends.
Inputs may be any that keep to these rules, and one draw needn't show every extreme that they name: `segment_tile_counts`: each row sums to 8. `adapter_pool_rows`: each pool row appears once.
All inputs are finite; a program needn't handle non-finite values.
Results may differ from the reference program's by a relative error of at most 0.0036.
Values may be sent and summed in bfloat16 or wider, within the bound.
A program may use at most 320 MiB of HBM per device.

```python
import math
import jax
import jax.numpy as jnp
import numpy as np
from jax import lax

MODEL_WIDTH = 8192
FF_W = 16384
ADAPTER_RANK = 128
TOKS = 1024
TILE = 128
SEGS = 3
TOKEN_GROUPS = 4
GROUP_DEVICES = 8
ADAPTER_POOL = 8
HIDDEN_SHARE_3 = 512
N_GRP = 4


def place_ends(values, key, least, largest):
    longest = values.shape.index(max(values.shape))
    spots = []
    for shift in (0, 1):
        where = [jax.random.randint(jax.random.fold_in(key, axis), (), 0, length) for axis, length in enumerate(values.shape)]
        where[longest] = (where[longest] + shift) % values.shape[longest]
        spots.append(tuple(where))
    return values.at[spots[0]].set(least).at[spots[1]].set(largest)


def levels(key, dims, cuts, low, top_value):
    def one(axis_at, shards_of):
        steps = jax.random.uniform(jax.random.fold_in(jax.random.fold_in(key, 6), axis_at), (shards_of,), jnp.float32, low / len(cuts), top_value / len(cuts))
        return jnp.repeat(jnp.exp(steps), dims[axis_at] // shards_of).reshape((-1,) + (1,) * (len(dims) - axis_at - 1))

    level = one(*cuts[0])
    for cut in cuts[1:]:
        level = level * one(*cut)
    return level


def split_up(number_of, total, most, slope):
    weights = [(1 << 20) // math.isqrt(rank ** slope) + 1 for rank in range(2, number_of + 1)]
    surplus, counts = total - most - (number_of - 1), [1] * (number_of - 1)
    while surplus > 0:
        candidates = [i for i in range(number_of - 1) if counts[i] < most]
        pool, budget = sum([weights[i] for i in candidates]), surplus
        for i in candidates:
            extra = min(most - counts[i], max(1, budget * weights[i] // pool), surplus)
            counts[i] = counts[i] + extra
            surplus = surplus - extra
    return np.array([most] + counts)


def uneven(rng, number_of, total, bound, slope):
    if number_of == 2:
        one = jax.random.randint(rng, (), max(1, total - bound), min(bound, total - 1) + 1)
        return jnp.stack([one, total - one])
    lengths = jnp.asarray(split_up(number_of, total, bound, slope), jnp.int32)
    couples = (number_of - 1) // 2
    giver, receiver = lengths[1:1 + 2 * couples:2], lengths[2:2 + 2 * couples:2]
    slack = jnp.minimum(giver - 1, bound - receiver)
    passed = jax.random.randint(jax.random.fold_in(rng, 1), (couples,), 0, 1 << 20) % (slack + 1)
    lengths = lengths.at[1:1 + 2 * couples:2].set(giver - passed).at[2:2 + 2 * couples:2].set(receiver + passed)
    return lengths[jax.random.permutation(jax.random.fold_in(rng, 2), number_of)]


def bell_draw(own_key, dims, scale, reach, cuts=(), kind=jnp.bfloat16):
    values = jax.random.normal(own_key, dims, jnp.float32) * scale
    if len(cuts) > 0:
        values = levels(own_key, dims, cuts, -0.22, 0.18) * values
    return jnp.clip(values, min=-reach, max=reach).astype(kind)


def setup_inputs(seed: int = 0) -> dict:
    seeds = jax.random.split(jax.random.key(seed), 8)
    return {
        "tokens": bell_draw(seeds[0], (TOKEN_GROUPS * TOKS, MODEL_WIDTH), 1.0, 6.0, ((0, 4), (1, 8))),
        "gate_up_weight": bell_draw(seeds[1], (MODEL_WIDTH, 2, FF_W), MODEL_WIDTH ** -0.5, 0.0625, ((2, 8),)),
        "down_factor_pool": bell_draw(seeds[2], (ADAPTER_POOL, MODEL_WIDTH, 2 * ADAPTER_RANK), MODEL_WIDTH ** -0.5, 0.0625, ((0, 8), (1, 4))),
        "up_factor_pool": bell_draw(seeds[3], (ADAPTER_POOL, TOKEN_GROUPS, GROUP_DEVICES, ADAPTER_RANK, 2 * HIDDEN_SHARE_3), ADAPTER_RANK ** -0.5, 0.5, ((0, 8), (1, 4))),
        "segment_adapters": place_ends(jax.random.randint(seeds[4], (TOKEN_GROUPS, SEGS), 0, ADAPTER_POOL), jax.random.fold_in(seeds[4], 1), 0, ADAPTER_POOL - 1).astype(jnp.int32),
        "segment_tile_counts": jax.vmap(lambda own: uneven(own, SEGS, TOKS // TILE, TOKS // TILE // 2, 1))(jax.random.split(seeds[5], TOKEN_GROUPS)).reshape((TOKEN_GROUPS, SEGS)).astype(jnp.int32),
        "adapter_pool_rows": jax.random.permutation(seeds[6], ADAPTER_POOL).astype(jnp.int32),
    }


adapter_scale = 0.5


def reference(tokens, gate_up_weight, down_factor_pool, up_factor_pool, segment_adapters, segment_tile_counts, adapter_pool_rows):
    tile_count = TOKS // TILE
    bounds = jnp.cumsum(segment_tile_counts, axis=1)
    positions = jnp.arange(tile_count, dtype=jnp.int32)
    tile_seg = jnp.sum((bounds[:, None, :] <= positions[None, :, None]).astype(jnp.int32), axis=2).astype(jnp.int32)
    tile_ids = jnp.take_along_axis(segment_adapters, tile_seg, axis=1)
    tile_rows = jnp.take(adapter_pool_rows, tile_ids.reshape(-1)).astype(jnp.int32)
    frozen_output = jnp.dot(tokens, gate_up_weight.reshape(MODEL_WIDTH, 2 * FF_W), preferred_element_type=jnp.float32)
    frozen_output = frozen_output.reshape(N_GRP * TOKS, 2, FF_W)
    token_tiles = tokens.reshape(N_GRP * tile_count, TILE, MODEL_WIDTH)

    def one_tile(item):
        token_rows_block, adapter_pool_row = item
        reduced_input = jnp.dot(token_rows_block, down_factor_pool[adapter_pool_row], preferred_element_type=jnp.float32).astype(jnp.bfloat16)
        expanded_output = up_factor_pool[adapter_pool_row].reshape(N_GRP, GROUP_DEVICES, ADAPTER_RANK, 2, HIDDEN_SHARE_3)
        expanded_output = jnp.transpose(expanded_output, (2, 3, 1, 0, 4)).reshape(ADAPTER_RANK, 2, FF_W)
        gate_part = jnp.dot(reduced_input[:, :ADAPTER_RANK], expanded_output[:, 0, :], preferred_element_type=jnp.float32)
        up_part = jnp.dot(reduced_input[:, ADAPTER_RANK:], expanded_output[:, 1, :], preferred_element_type=jnp.float32)
        return jnp.stack([gate_part, up_part], axis=1)

    adapted_output = lax.map(one_tile, (token_tiles, tile_rows)).reshape(N_GRP * TOKS, 2, FF_W)
    gate_combined = frozen_output[:, 0, :] + adapter_scale * adapted_output[:, 0, :]
    up_combined = frozen_output[:, 1, :] + adapter_scale * adapted_output[:, 1, :]
    return (jax.nn.silu(gate_combined) * up_combined).astype(jnp.bfloat16)
```

```python
import functools

import jax
import jax.numpy as jnp
from jax import lax
from jax.experimental import pallas as pl
from jax.experimental.pallas import tpu as pltpu
from jax.sharding import PartitionSpec as P


TILE = 128
VMEM_LIMIT = 60 * 1024 * 1024

adapter_scale = 0.5


TP = ("tp", "cores")


def tile_segments(tile_lengths, tile_count):
    bounds = jnp.cumsum(tile_lengths)
    positions = jnp.arange(tile_count, dtype=jnp.int32)
    return jnp.sum((bounds[None, :] <= positions[:, None]).astype(jnp.int32), axis=1)


def ring_device(position, tp_size, cores_size):
    c = position // tp_size
    t = position % tp_size
    t = t + (c % 2) * (tp_size - 1 - 2 * t)
    return t * cores_size + c


def ring_position(tp_index, cores_index, tp_size):
    t = tp_index + (cores_index % 2) * (tp_size - 1 - 2 * tp_index)
    return cores_index * tp_size + t


def partial_kernel(count, with_acc, rows_ref, *refs):
    xs, ws = refs[:count], refs[count : 2 * count]
    out = refs[-1]
    ws = [jnp.swapaxes(w[...], 0, 1) for w in ws]
    for h in range(2):
        total = refs[2 * count][h] if with_acc else None
        for x, w in zip(xs, ws):
            term = jnp.dot(x[...], w[h], preferred_element_type=jnp.float32)
            total = term if total is None else total + term
        out[h] = total


def partial_matmul(xs, weight, rows, acc, block_cols):
    count = len(xs)
    tokens, depth = xs[0].shape
    hidden = weight.shape[2]
    block_cols = min(block_cols, 256)
    in_specs = [pl.BlockSpec((tokens, depth), lambda j, r: (0, 0))] * count
    for k in range(count):
        in_specs.append(
            pl.BlockSpec((depth, 2, block_cols), lambda j, r, k=k: (r[k], 0, j))
        )
    acc_spec = pl.BlockSpec((2, tokens, block_cols), lambda j, r: (0, 0, j))
    operands = list(xs) + [weight] * count
    aliases = {}
    if acc is not None:
        in_specs.append(acc_spec)
        aliases = {1 + len(operands): 0}
        operands.append(acc)
    return pl.pallas_call(
        functools.partial(partial_kernel, count, acc is not None),
        out_shape=jax.ShapeDtypeStruct((2, tokens, hidden), jnp.float32),
        grid_spec=pltpu.PrefetchScalarGridSpec(
            num_scalar_prefetch=1,
            grid=(hidden // block_cols,),
            in_specs=in_specs,
            out_specs=acc_spec,
        ),
        input_output_aliases=aliases,
        compiler_params=pltpu.CompilerParams(vmem_limit_bytes=VMEM_LIMIT),
        cost_estimate=pl.CostEstimate(
            flops=4 * count * tokens * depth * hidden,
            bytes_accessed=count * 4 * depth * hidden + 16 * tokens * hidden,
            transcendentals=0,
        ),
    )(rows, *operands)


def final_kernel(tiles_per_half, rank, rows_ref, seg_ref, xt, xb, w, acc, shrunk, b, out, total):
    narrow = out.shape[1]
    w = jnp.swapaxes(w[...], 0, 1)
    for p, x in enumerate((xt, xb)):
        for h in range(2):
            span = slice(p * x.shape[0], (p + 1) * x.shape[0])
            total[h, span] = acc[h, span] + jnp.dot(
                x[...], w[h], preferred_element_type=jnp.float32
            )
        for t in range(p * tiles_per_half, (p + 1) * tiles_per_half):
            seg = seg_ref[t]
            span = slice(t * TILE, (t + 1) * TILE)
            both = []
            for h in range(2):
                delta = jnp.dot(
                    shrunk[span, h * rank : (h + 1) * rank],
                    b[0, seg, :, h * narrow : (h + 1) * narrow],
                    preferred_element_type=jnp.float32,
                )
                both.append(total[h, span] + adapter_scale * delta)
            gate, up = both
            out[span] = (gate / (1.0 + jnp.exp(-gate)) * up).astype(out.dtype)


def final_matmul(xt, xb, weight, rows, acc, shrunk, b_chosen, tile_seg):
    half, depth = xt.shape
    tokens = 2 * half
    hidden = weight.shape[2]
    blocks, segs, rank, twice = b_chosen.shape
    narrow = twice // 2
    return pl.pallas_call(
        functools.partial(final_kernel, half // TILE, rank),
        out_shape=jax.ShapeDtypeStruct((tokens, hidden), jnp.bfloat16),
        grid_spec=pltpu.PrefetchScalarGridSpec(
            num_scalar_prefetch=2,
            grid=(blocks,),
            in_specs=[
                pl.BlockSpec((half, depth), lambda j, r, s: (0, 0)),
                pl.BlockSpec((half, depth), lambda j, r, s: (0, 0)),
                pl.BlockSpec((depth, 2, narrow), lambda j, r, s: (r[0], 0, j)),
                pl.BlockSpec((2, tokens, narrow), lambda j, r, s: (0, 0, j)),
                pl.BlockSpec((tokens, 2 * rank), lambda j, r, s: (0, 0)),
                pl.BlockSpec((1, segs, rank, twice), lambda j, r, s: (j, 0, 0, 0)),
            ],
            out_specs=pl.BlockSpec((tokens, narrow), lambda j, r, s: (0, j)),
            scratch_shapes=[pltpu.VMEM((2, tokens, narrow), jnp.float32)],
        ),
        compiler_params=pltpu.CompilerParams(vmem_limit_bytes=VMEM_LIMIT),
        cost_estimate=pl.CostEstimate(
            flops=4 * tokens * (depth + rank) * hidden,
            bytes_accessed=4 * depth * hidden + 10 * tokens * hidden,
            transcendentals=tokens * hidden,
        ),
    )(rows, tile_seg, xt, xb, weight, acc, shrunk, b_chosen)


def group_exchange(pool, slots):
    groups = lax.axis_size("grp")
    g = lax.axis_index("grp")
    parts = []
    for k in range(groups):
        wanted = lax.dynamic_index_in_dim(slots, (g + k) % groups, 0, keepdims=False)
        part = jnp.take(pool, wanted, axis=0, mode="clip")
        if k:
            pairs = [(i, (i + k) % groups) for i in range(groups)]
            part = lax.ppermute(part, "grp", pairs)
        parts.append(part)
    sources = (g + groups - jnp.arange(groups)) % groups
    return jnp.take(jnp.stack(parts), sources, axis=0, mode="clip")


MESH = pl.DeviceIdType.MESH
CHUNKS = 4
END_SHIFT = 1
BLOCK_COLS = 256


def table(rows, i, k):
    total = 0
    for a, row in enumerate(rows):
        for b, value in enumerate(row):
            if value:
                total = total + jnp.where((i == a) & (k == b), value, 0)
    return total


def reach(size):
    return [sorted(range(size), key=lambda t, z=z: (abs(t - z), t)) for z in range(size)]


def shifted(size, source, dest, c):
    to_end = ((dest == 0) | (dest == size - 1)) & (c >= CHUNKS - END_SHIFT)
    from_end = (source == 0) | (source == size - 1)
    return to_end | from_end


def gather_kernel(
    tile_rows,
    tokens,
    weight,
    down,
    up,
    xg,
    u_all,
    shrunk,
    acc_out,
    acc,
    xv,
    wbuf,
    d0,
    d_all,
    part,
    sums,
    own,
    recv,
    up_sem,
    dn_sem,
    y_sem,
    x_sem,
    w_sem,
    d0_send,
    d0_recv,
    d1_send,
    d1_recv,
    d2_send,
    d2_recv,
    u1_send,
    u1_recv,
    u2_send,
    u2_recv,
    s1_send,
    s1_recv,
    s2_send,
    s2_recv,
    o_sem,
):
    groups = lax.axis_size("grp")
    size, cores = lax.axis_size("tp"), lax.axis_size("cores")
    n = size * cores
    g, z, y = lax.axis_index("grp"), lax.axis_index("tp"), lax.axis_index("cores")
    me = z * cores + y
    other = 1 - y
    token_count, depth = tokens.shape
    rows = token_count // CHUNKS
    hidden = weight.shape[2]
    cols = wbuf.shape[-1]
    blocks = hidden // cols
    per = n // groups
    share = token_count // n
    order = reach(size)

    def peer(k):
        return {"grp": lax.rem(g + k, groups)}

    def mate(k):
        p = lax.rem(me + k, n)
        return p, {"tp": p // cores, "cores": lax.rem(p, cores)}

    def span(c):
        if isinstance(c, int):
            return pl.ds(c * rows, rows)
        return pl.ds(pl.multiple_of(c * rows, rows), rows)

    def hop(src, s, c, sems, dev):
        return pltpu.make_async_remote_copy(
            src_ref=src,
            dst_ref=xg.at[s, span(c)],
            send_sem=sems.at[s, c],
            recv_sem=recv.at[s, c],
            device_id=dev,
            device_id_type=MESH,
        )

    up_dev, dn_dev, y_dev = {"tp": z + 1}, {"tp": z - 1}, {"cores": other}

    def arrived(s, c):
        hop(xg.at[s, span(c)], s, c, y_sem, y_dev).wait_recv()

    def forward(s, c, sems, dev):
        hop(xg.at[s, span(c)], s, c, sems, dev).start()

    def send_own(c):
        src = tokens.at[span(c)]

        @pl.when(z + 1 < size)
        def _():
            hop(src, me, c, up_sem, up_dev).start()

        @pl.when(z >= 1)
        def _():
            hop(src, me, c, dn_sem, dn_dev).start()

        hop(src, me, c, y_sem, y_dev).start()

    def row_arrival(r, c, first):
        lo, hi = z - r, z + r

        @pl.when(lo >= 0)
        def _():
            s = lo * cores + y
            arrived(s, c)

            @pl.when(z + 1 < size)
            def _():
                forward(s, c, up_sem, up_dev)

            @pl.when(jnp.logical_not(shifted(size, lo, z, c)) if first else z >= 0)
            def _():
                forward(s, c, y_sem, y_dev)

        @pl.when(hi < size)
        def _():
            s = hi * cores + y
            arrived(s, c)

            @pl.when(z >= 1)
            def _():
                forward(s, c, dn_sem, dn_dev)

            @pl.when(jnp.logical_not(shifted(size, hi, z, c)) if first else z >= 0)
            def _():
                forward(s, c, y_sem, y_dev)

    def cross_arrival(r, c):
        lo, hi = z - r, z + r

        @pl.when(lo >= 0)
        def _():
            arrived(lo * cores + other, c)

        @pl.when(hi < size)
        def _():
            arrived(hi * cores + other, c)

    def mate_arrival(c):
        s = z * cores + other
        arrived(s, c)

        @pl.when((z + 1 < size) & shifted(size, z, z + 1, c))
        def _():
            forward(s, c, up_sem, up_dev)

        @pl.when((z >= 1) & shifted(size, z, z - 1, c))
        def _():
            forward(s, c, dn_sem, dn_dev)

    def w_copy(piece, j, slot, k):
        return pltpu.make_async_copy(
            weight.at[
                pl.ds(pl.multiple_of(piece * depth, depth), depth),
                slice(None),
                pl.ds(pl.multiple_of(j * cols, cols), cols),
            ],
            wbuf.at[slot, k],
            w_sem.at[slot, k],
        )

    def x_copy(src, k):
        return pltpu.make_async_copy(src, xv.at[k], x_sem.at[k])

    def multiply(pieces, j, count, first):
        slot = lax.rem(j, 2)

        @pl.when(j + 1 < blocks)
        def _():
            for k, piece in enumerate(pieces):
                w_copy(piece, j + 1, 1 - slot, k).start()

        where = pl.ds(pl.multiple_of(j * cols, cols), cols)
        for k, piece in enumerate(pieces):
            w_copy(piece, j, slot, k).wait()
        ws = [jnp.swapaxes(wbuf[slot, k], 0, 1) for k in range(len(pieces))]
        for h in range(2):
            total = None if first else acc[h, pl.ds(0, count), where]
            for k in range(len(pieces)):
                term = jnp.dot(
                    xv[k, pl.ds(0, count)], ws[k][h], preferred_element_type=jnp.float32
                )
                total = term if total is None else total + term
            acc[h, pl.ds(0, count), where] = total

    def first_tiles(pieces):
        for k, piece in enumerate(pieces):
            w_copy(piece, 0, 0, k).start()

    def exchange(k, src, dst, sends, recvs, dev):
        return pltpu.make_async_remote_copy(
            src_ref=src,
            dst_ref=dst,
            send_sem=sends.at[k],
            recv_sem=recvs.at[k],
            device_id=dev,
            device_id_type=MESH,
        )

    def d0_copy(k):
        return exchange(
            k, down.at[:, lax.rem(g + k, groups)], d0.at[g], d0_send, d0_recv, peer(k)
        )

    def d1_copy(k):
        p, dev = mate(k)
        return exchange(
            k, d0.at[p // per, lax.rem(p, per)], d_all.at[g, me], d1_send, d1_recv, dev
        )

    def d2_copy(k):
        return exchange(k, d_all.at[g], d_all.at[g], d2_send, d2_recv, peer(k))

    def u1_copy(k):
        p, dev = mate(k)
        return exchange(k, up.at[p], u_all.at[g, me], u1_send, u1_recv, dev)

    def u2_copy(k):
        return exchange(k, u_all.at[g], u_all.at[g], u2_send, u2_recv, peer(k))

    def s1_copy(k):
        p, dev = mate(k)
        src = part.at[pl.ds(pl.multiple_of(p * share, share), share)]
        return exchange(k, src, sums.at[me], s1_send, s1_recv, dev)

    def s2_copy(k):
        _, dev = mate(k)
        return exchange(k, own, shrunk.at[me], s2_send, s2_recv, dev)

    def here(src, dst, k):
        return pltpu.make_async_copy(src, dst, o_sem.at[k])

    for k in range(1, groups):
        d0_copy(k).start()
    here(down.at[:, g], d0.at[g], 0).start()
    x_copy(tokens, 0).start()
    first_tiles([me])
    send_own(0)
    here(down.at[:, g], d0.at[g], 0).wait()
    for k in range(1, groups):
        d0_copy(k).wait_recv()
    for k in range(1, n):
        d1_copy(k).start()
    here(d0.at[me // per, lax.rem(me, per)], d_all.at[g, me], 1).start()
    for c in range(1, CHUNKS):
        send_own(c)
    for k in range(1, n):
        u1_copy(k).start()
    here(up.at[me], u_all.at[g, me], 2).start()
    x_copy(tokens, 0).wait()

    step = blocks // CHUNKS

    def first_round(c, carry):
        row_arrival(1, c, True)
        mate_arrival(c)
        for i in range(step):
            multiply([me], c * step + i, token_count, True)
        return carry

    lax.fori_loop(0, CHUNKS, first_round, 0)

    here(d0.at[me // per, lax.rem(me, per)], d_all.at[g, me], 1).wait()
    for k in range(1, n):
        d1_copy(k).wait_recv()
    for k in range(1, groups):
        d2_copy(k).start()
    here(up.at[me], u_all.at[g, me], 2).wait()
    for k in range(1, n):
        u1_copy(k).wait_recv()
    for k in range(1, groups):
        u2_copy(k).start()

    def later_round(r, carry):
        pieces = [
            table(order, z, r - 1) * cores + y,
            table(order, z, r - 2) * cores + other,
        ]
        for k in range(2):
            x_copy(xg.at[pieces[k]], k).start()
        first_tiles(pieces)
        for k in range(2):
            x_copy(xg.at[pieces[k]], k).wait()

        def body(c, carry):
            @pl.when(r < size)
            def _():
                row_arrival(r, c, False)
                cross_arrival(r - 1, c)

            for i in range(step):
                multiply(pieces, c * step + i, token_count, False)
            return carry

        lax.fori_loop(0, CHUNKS, body, 0)

        @pl.when(r == 2)
        def _():
            for k in range(1, groups):
                d2_copy(k).wait_recv()
            x_copy(tokens, 0).start()
            x_copy(tokens, 0).wait()

            def one_tile(t, carry):
                q = tile_rows[t]
                where = pl.ds(pl.multiple_of(t * TILE, TILE), TILE)
                piece = depth // groups
                total = None
                for j in range(groups):
                    term = jnp.dot(
                        xv[0, where, j * piece : (j + 1) * piece],
                        d_all[j, q],
                        preferred_element_type=jnp.float32,
                    )
                    total = term if total is None else total + term
                part[where] = total.astype(part.dtype)
                return carry

            lax.fori_loop(0, token_count // TILE, one_tile, 0)
            for k in range(1, n):
                s1_copy(k).start()

        @pl.when(r == 3)
        def _():
            for k in range(1, n):
                s1_copy(k).wait_recv()
            mine = part[pl.ds(pl.multiple_of(me * share, share), share)].astype(jnp.float32)
            for k in range(1, n):
                mine = mine + sums[lax.rem(me + k, n)].astype(jnp.float32)
            own[...] = mine.astype(own.dtype)
            here(own, shrunk.at[me], 3).start()
            for k in range(1, n):
                s2_copy(k).start()

        return carry

    lax.fori_loop(2, size + 1, later_round, 0)

    last = table(order, z, size - 1) * cores + other
    count = token_count - rows
    first_tiles([last])
    for c in range(CHUNKS - 1):
        cross_arrival(size - 1, c)
    last_x = pltpu.make_async_copy(
        xg.at[last, pl.ds(0, count)], xv.at[0, pl.ds(0, count)], x_sem.at[0]
    )
    last_x.start()
    last_x.wait()

    def acc_copy(j):
        where = pl.ds(pl.multiple_of(j * cols, cols), cols)
        return pltpu.make_async_copy(
            acc.at[:, :, where], acc_out.at[:, :, where], o_sem.at[4 + j]
        )

    def last_round(j, carry):
        multiply([last], j, count, False)
        acc_copy(j).start()
        return carry

    lax.fori_loop(0, blocks, last_round, 0)

    here(own, shrunk.at[me], 3).wait()
    for k in range(1, n):
        s2_copy(k).wait_recv()
    for k in range(1, groups):
        u2_copy(k).wait_recv()
    for k in range(1, groups):
        d0_copy(k).wait_send()
        d2_copy(k).wait_send()
        u2_copy(k).wait_send()
    for k in range(1, n):
        d1_copy(k).wait_send()
        u1_copy(k).wait_send()
        s1_copy(k).wait_send()
        s2_copy(k).wait_send()

    def drain(i, carry):
        t, c = i // CHUNKS, lax.rem(i, CHUNKS)
        s, across = t * cores + y, t * cores + other

        def sent(s, sems, dev):
            hop(xg.at[s, span(c)], s, c, sems, dev).wait_send()

        @pl.when((z + 1 < size) & (t <= z))
        def _():
            sent(s, up_sem, up_dev)

        @pl.when((z >= 1) & (t >= z))
        def _():
            sent(s, dn_sem, dn_dev)

        near = (t == z - 1) | (t == z + 1)

        @pl.when(jnp.logical_not(near & shifted(size, t, z, c)))
        def _():
            sent(s, y_sem, y_dev)

        @pl.when((t == z) & (z + 1 < size) & shifted(size, z, z + 1, c))
        def _():
            sent(across, up_sem, up_dev)

        @pl.when((t == z) & (z >= 1) & shifted(size, z, z - 1, c))
        def _():
            sent(across, dn_sem, dn_dev)

        return carry

    lax.fori_loop(0, size * CHUNKS, drain, 0)

    def acc_done(j, carry):
        acc_copy(j).wait()
        return carry

    lax.fori_loop(0, blocks, acc_done, 0)
    cross_arrival(size - 1, CHUNKS - 1)


def gather_matmul(tile_rows, tokens, weight, down, up, groups, n):
    token_count, depth = tokens.shape
    hidden = weight.shape[2]
    cols = min(BLOCK_COLS, hidden)
    twice_rank = down.shape[-1]
    share = token_count // n
    dma = pltpu.SemaphoreType.DMA
    any_space = pl.BlockSpec(memory_space=pl.ANY)
    return pl.pallas_call(
        gather_kernel,
        out_shape=(
            jax.ShapeDtypeStruct((n, token_count, depth), tokens.dtype),
            jax.ShapeDtypeStruct((groups,) + up.shape, up.dtype),
            jax.ShapeDtypeStruct((n, share, twice_rank), jnp.bfloat16),
            jax.ShapeDtypeStruct((2, token_count, hidden), jnp.float32),
        ),
        in_specs=[pl.BlockSpec(memory_space=pltpu.SMEM)] + [any_space] * 4,
        out_specs=(any_space,) * 4,
        scratch_shapes=[
            pltpu.VMEM((2, token_count, hidden), jnp.float32),
            pltpu.VMEM((2, token_count, depth), tokens.dtype),
            pltpu.VMEM((2, 2, depth, 2, cols), weight.dtype),
            pltpu.VMEM((groups, n // groups) + down.shape[2:], down.dtype),
            pltpu.VMEM((groups, n) + down.shape[2:], down.dtype),
            pltpu.VMEM((token_count, twice_rank), jnp.bfloat16),
            pltpu.VMEM((n, share, twice_rank), jnp.bfloat16),
            pltpu.VMEM((share, twice_rank), jnp.bfloat16),
            dma((n, CHUNKS)),
            dma((n, CHUNKS)),
            dma((n, CHUNKS)),
            dma((n, CHUNKS)),
            dma((2,)),
            dma((2, 2)),
            dma((groups,)),
            dma((groups,)),
            dma((n,)),
            dma((n,)),
            dma((groups,)),
            dma((groups,)),
            dma((n,)),
            dma((n,)),
            dma((groups,)),
            dma((groups,)),
            dma((n,)),
            dma((n,)),
            dma((n,)),
            dma((n,)),
            dma((4 + hidden // cols,)),
        ],
        compiler_params=pltpu.CompilerParams(
            vmem_limit_bytes=VMEM_LIMIT, has_side_effects=True
        ),
        name="gather_matmul",
    )(tile_rows, tokens, weight, down, up)


def finish_kernel(rank, last_ref, tile_rows, x, w, acc, shrunk, b, out):
    token_count, narrow = out.shape
    rows = x.shape[1]
    start = token_count - rows
    w = jnp.swapaxes(w[...], 0, 1)
    tail = [
        acc[h, start:] + jnp.dot(x[0], w[h], preferred_element_type=jnp.float32)
        for h in range(2)
    ]
    for t in range(token_count // TILE):
        q = tile_rows[t]
        span = slice(t * TILE, (t + 1) * TILE)
        both = []
        for h in range(2):
            delta = jnp.dot(
                shrunk[span, h * rank : (h + 1) * rank],
                b[0, q, :, h * narrow : (h + 1) * narrow],
                preferred_element_type=jnp.float32,
            )
            if t * TILE >= start:
                total = tail[h][t * TILE - start : (t + 1) * TILE - start]
            else:
                total = acc[h, span]
            both.append(total + adapter_scale * delta)
        gate, lift = both
        out[span] = (gate / (1.0 + jnp.exp(-gate)) * lift).astype(out.dtype)


def finish(last, tile_rows, xg, weight, acc, shrunk, u_all):
    _, token_count, depth = xg.shape
    hidden = weight.shape[2]
    groups, pool, rank, twice = u_all.shape
    narrow = twice // 2
    rows = token_count // CHUNKS
    return pl.pallas_call(
        functools.partial(finish_kernel, rank),
        out_shape=jax.ShapeDtypeStruct((token_count, hidden), jnp.bfloat16),
        grid_spec=pltpu.PrefetchScalarGridSpec(
            num_scalar_prefetch=2,
            grid=(groups,),
            in_specs=[
                pl.BlockSpec((1, rows, depth), lambda j, s, q: (s[0], CHUNKS - 1, 0)),
                pl.BlockSpec((depth, 2, narrow), lambda j, s, q: (s[0], 0, j)),
                pl.BlockSpec((2, token_count, narrow), lambda j, s, q: (0, 0, j)),
                pl.BlockSpec((token_count, 2 * rank), lambda j, s, q: (0, 0)),
                pl.BlockSpec((1, pool, rank, twice), lambda j, s, q: (j, 0, 0, 0)),
            ],
            out_specs=pl.BlockSpec((token_count, narrow), lambda j, s, q: (0, j)),
        ),
        compiler_params=pltpu.CompilerParams(vmem_limit_bytes=VMEM_LIMIT),
        name="finish",
    )(last, tile_rows, xg, weight, acc, shrunk, u_all)


def compute_fused(
    tokens,
    gate_up_weight,
    down_factor_pool,
    up_factor_pool,
    segment_adapters,
    segment_tile_counts,
    adapter_pool_rows,
):
    groups = lax.axis_size("grp")
    tp_size, cores_size = lax.axis_size("tp"), lax.axis_size("cores")
    n = tp_size * cores_size
    token_count, depth = tokens.shape
    twice_rank = down_factor_pool.shape[2]
    g, z, y = lax.axis_index("grp"), lax.axis_index("tp"), lax.axis_index("cores")
    tile_count = token_count // TILE
    tile_seg = tile_segments(segment_tile_counts[0], tile_count)
    mine = lax.dynamic_index_in_dim(segment_adapters, g, 0, keepdims=False)
    tile_adapter = jnp.take(mine, tile_seg, mode="clip")
    tile_rows = jnp.take(adapter_pool_rows, tile_adapter, mode="clip").astype(jnp.int32)
    down = down_factor_pool.reshape(n // groups, groups, depth // groups, twice_rank)
    up = up_factor_pool.reshape(up_factor_pool.shape[2:])
    xg, u_all, shrunk, acc = gather_matmul(
        tile_rows, tokens, gate_up_weight, down, up, groups, n
    )
    far = jnp.asarray([row[-1] for row in reach(tp_size)], jnp.int32)[z]
    last = (far * cores_size + (1 - y)).astype(jnp.int32)[None]
    return finish(
        last,
        tile_rows,
        xg,
        gate_up_weight,
        acc,
        shrunk.reshape(token_count, twice_rank),
        u_all,
    )


def fits(mesh):
    size, cores, groups = mesh.shape["tp"], mesh.shape["cores"], mesh.shape["grp"]
    return cores == 2 and 3 <= size <= 4 and (size * cores) % groups == 0


def per_device(*args):
    return compute(*args)


def compute(
    tokens,
    gate_up_weight,
    down_factor_pool,
    up_factor_pool,
    segment_adapters,
    segment_tile_counts,
    adapter_pool_rows,
):
    groups = lax.axis_size("grp")
    tp_size, cores_size = lax.axis_size("tp"), lax.axis_size("cores")
    n = tp_size * cores_size
    token_count, depth = tokens.shape
    local_hidden_width = gate_up_weight.shape[2]
    twice_rank = down_factor_pool.shape[2]
    narrow = local_hidden_width // groups
    seg_count = segment_adapters.shape[1]
    half = token_count // 2

    me = ring_position(lax.axis_index("tp"), lax.axis_index("cores"), tp_size)
    order = [ring_device(k, tp_size, cores_size) for k in range(n)]
    forward = [(order[k], order[(k + 1) % n]) for k in range(n)]
    backward = [(order[(k + 1) % n], order[k]) for k in range(n)]

    def owner(shift):
        return ring_device((me + shift + n) % n, tp_size, cores_size).astype(jnp.int32)

    full_steps = (n - 1) // 2
    lefts, rights = [tokens], [tokens]
    for _ in range(1, full_steps + 1):
        lefts.append(lax.ppermute(lefts[-1], TP, forward))
        rights.append(lax.ppermute(rights[-1], TP, backward))
    last_top = lax.ppermute(lefts[-1][:half], TP, forward)
    last_bottom = lax.ppermute(rights[-1][half:], TP, backward)

    piece = depth // groups
    a = down_factor_pool.reshape(n // groups, groups, piece, twice_rank)
    a = lax.all_to_all(a, "grp", split_axis=1, concat_axis=0, tiled=True)
    a = a.reshape(n, piece, twice_rank)
    a = lax.all_to_all(a, TP, split_axis=0, concat_axis=0, tiled=True)
    b = up_factor_pool.reshape(up_factor_pool.shape[2:])
    b = lax.all_to_all(b, TP, split_axis=0, concat_axis=0, tiled=True)
    slots = jnp.take(adapter_pool_rows, segment_adapters, mode="clip")
    a = group_exchange(a, slots)
    b = group_exchange(b, slots)
    block_cols = narrow
    if narrow % 128:
        block_cols = local_hidden_width
        b = b.reshape(groups, seg_count, b.shape[2], 2, narrow)
        b = jnp.transpose(b, (1, 2, 3, 0, 4))
        b = b.reshape(1, seg_count, b.shape[1], 2 * block_cols)

    tile_count = token_count // TILE
    tile_seg = tile_segments(segment_tile_counts[0], tile_count).astype(jnp.int32)
    row_seg = jnp.repeat(tile_seg, TILE)[:, None]
    partial = None
    for j in range(seg_count):
        term = jnp.dot(
            tokens, a[:, j].reshape(depth, twice_rank), preferred_element_type=jnp.float32
        )
        partial = term if partial is None else jnp.where(row_seg == j, term, partial)
    share = token_count // n
    partial = lax.all_to_all(
        partial.reshape(n, share, twice_rank), TP, split_axis=0, concat_axis=0, tiled=True
    )
    own = jnp.sum(partial, axis=0).astype(jnp.bfloat16)
    shrunk = lax.all_to_all(
        jnp.broadcast_to(own[None], (n, share, twice_rank)),
        TP,
        split_axis=0,
        concat_axis=0,
        tiled=True,
    ).reshape(token_count, twice_rank)

    acc = None
    for s in range(1, full_steps + 1):
        xs = [lefts[s], rights[s]]
        rows = [owner(-s), owner(s)]
        if s == 1:
            xs.insert(0, tokens)
            rows.insert(0, owner(0))
        acc = partial_matmul(xs, gate_up_weight, jnp.stack(rows), acc, block_cols)
    return final_matmul(
        last_top, last_bottom, gate_up_weight, jnp.stack([owner(n // 2)]), acc, shrunk, b, tile_seg
    )


def fused(*args):
    return compute_fused(*args)


def solution(mesh):
    direct = fits(mesh)
    return jax.shard_map(
        fused if direct else per_device,
        mesh=mesh,
        in_specs=(
            P("grp", ("tp", "cores")),
            P(None, None, ("tp", "cores")),
            P(("tp", "cores"), "grp", None),
            P(("tp", "cores"), "grp", None, None, None),
            P(),
            P("grp", None),
            P(),
        ),
        out_specs=P("grp", ("tp", "cores")),
        check_vma=False,
    )
```

```python
import functools

import jax
import jax.numpy as jnp
from jax import lax
from jax.experimental import pallas as pl
from jax.experimental.pallas import tpu as pltpu
from jax.sharding import PartitionSpec as P


TILE = 128
VMEM_LIMIT = 60 * 1024 * 1024

adapter_scale = 0.5


TP = ("tp", "cores")


def tile_segments(tile_lengths, tile_count):
    bounds = jnp.cumsum(tile_lengths)
    positions = jnp.arange(tile_count, dtype=jnp.int32)
    return jnp.sum((bounds[None, :] <= positions[:, None]).astype(jnp.int32), axis=1)


def ring_device(position, tp_size, cores_size):
    c = position // tp_size
    t = position % tp_size
    t = t + (c % 2) * (tp_size - 1 - 2 * t)
    return t * cores_size + c


def ring_position(tp_index, cores_index, tp_size):
    t = tp_index + (cores_index % 2) * (tp_size - 1 - 2 * tp_index)
    return cores_index * tp_size + t


def partial_kernel(count, with_acc, rows_ref, *refs):
    xs, ws = refs[:count], refs[count : 2 * count]
    out = refs[-1]
    ws = [jnp.swapaxes(w[...], 0, 1) for w in ws]
    for h in range(2):
        total = refs[2 * count][h] if with_acc else None
        for x, w in zip(xs, ws):
            term = jnp.dot(x[...], w[h], preferred_element_type=jnp.float32)
            total = term if total is None else total + term
        out[h] = total


def partial_matmul(xs, weight, rows, acc, block_cols):
    count = len(xs)
    tokens, depth = xs[0].shape
    hidden = weight.shape[2]
    block_cols = min(block_cols, 256)
    in_specs = [pl.BlockSpec((tokens, depth), lambda j, r: (0, 0))] * count
    for k in range(count):
        in_specs.append(
            pl.BlockSpec((depth, 2, block_cols), lambda j, r, k=k: (r[k], 0, j))
        )
    acc_spec = pl.BlockSpec((2, tokens, block_cols), lambda j, r: (0, 0, j))
    operands = list(xs) + [weight] * count
    aliases = {}
    if acc is not None:
        in_specs.append(acc_spec)
        aliases = {1 + len(operands): 0}
        operands.append(acc)
    return pl.pallas_call(
        functools.partial(partial_kernel, count, acc is not None),
        out_shape=jax.ShapeDtypeStruct((2, tokens, hidden), jnp.float32),
        grid_spec=pltpu.PrefetchScalarGridSpec(
            num_scalar_prefetch=1,
            grid=(hidden // block_cols,),
            in_specs=in_specs,
            out_specs=acc_spec,
        ),
        input_output_aliases=aliases,
        compiler_params=pltpu.CompilerParams(vmem_limit_bytes=VMEM_LIMIT),
        cost_estimate=pl.CostEstimate(
            flops=4 * count * tokens * depth * hidden,
            bytes_accessed=count * 4 * depth * hidden + 16 * tokens * hidden,
            transcendentals=0,
        ),
    )(rows, *operands)


def final_kernel(tiles_per_half, rank, rows_ref, seg_ref, xt, xb, w, acc, shrunk, b, out, total):
    narrow = out.shape[1]
    w = jnp.swapaxes(w[...], 0, 1)
    for p, x in enumerate((xt, xb)):
        for h in range(2):
            span = slice(p * x.shape[0], (p + 1) * x.shape[0])
            total[h, span] = acc[h, span] + jnp.dot(
                x[...], w[h], preferred_element_type=jnp.float32
            )
        for t in range(p * tiles_per_half, (p + 1) * tiles_per_half):
            seg = seg_ref[t]
            span = slice(t * TILE, (t + 1) * TILE)
            both = []
            for h in range(2):
                delta = jnp.dot(
                    shrunk[span, h * rank : (h + 1) * rank],
                    b[0, seg, :, h * narrow : (h + 1) * narrow],
                    preferred_element_type=jnp.float32,
                )
                both.append(total[h, span] + adapter_scale * delta)
            gate, up = both
            out[span] = (gate / (1.0 + jnp.exp(-gate)) * up).astype(out.dtype)


def final_matmul(xt, xb, weight, rows, acc, shrunk, b_chosen, tile_seg):
    half, depth = xt.shape
    tokens = 2 * half
    hidden = weight.shape[2]
    blocks, segs, rank, twice = b_chosen.shape
    narrow = twice // 2
    return pl.pallas_call(
        functools.partial(final_kernel, half // TILE, rank),
        out_shape=jax.ShapeDtypeStruct((tokens, hidden), jnp.bfloat16),
        grid_spec=pltpu.PrefetchScalarGridSpec(
            num_scalar_prefetch=2,
            grid=(blocks,),
            in_specs=[
                pl.BlockSpec((half, depth), lambda j, r, s: (0, 0)),
                pl.BlockSpec((half, depth), lambda j, r, s: (0, 0)),
                pl.BlockSpec((depth, 2, narrow), lambda j, r, s: (r[0], 0, j)),
                pl.BlockSpec((2, tokens, narrow), lambda j, r, s: (0, 0, j)),
                pl.BlockSpec((tokens, 2 * rank), lambda j, r, s: (0, 0)),
                pl.BlockSpec((1, segs, rank, twice), lambda j, r, s: (j, 0, 0, 0)),
            ],
            out_specs=pl.BlockSpec((tokens, narrow), lambda j, r, s: (0, j)),
            scratch_shapes=[pltpu.VMEM((2, tokens, narrow), jnp.float32)],
        ),
        compiler_params=pltpu.CompilerParams(vmem_limit_bytes=VMEM_LIMIT),
        cost_estimate=pl.CostEstimate(
            flops=4 * tokens * (depth + rank) * hidden,
            bytes_accessed=4 * depth * hidden + 10 * tokens * hidden,
            transcendentals=tokens * hidden,
        ),
    )(rows, tile_seg, xt, xb, weight, acc, shrunk, b_chosen)


def group_exchange(pool, slots):
    groups = lax.axis_size("grp")
    g = lax.axis_index("grp")
    parts = []
    for k in range(groups):
        wanted = lax.dynamic_index_in_dim(slots, (g + k) % groups, 0, keepdims=False)
        part = jnp.take(pool, wanted, axis=0, mode="clip")
        if k:
            pairs = [(i, (i + k) % groups) for i in range(groups)]
            part = lax.ppermute(part, "grp", pairs)
        parts.append(part)
    sources = (g + groups - jnp.arange(groups)) % groups
    return jnp.take(jnp.stack(parts), sources, axis=0, mode="clip")


MESH = pl.DeviceIdType.MESH
CHUNKS = 4
END_SHIFT = 0
BLOCK_COLS = 256


def table(rows, i, k):
    total = 0
    for a, row in enumerate(rows):
        for b, value in enumerate(row):
            if value:
                total = total + jnp.where((i == a) & (k == b), value, 0)
    return total


def reach(size):
    return [sorted(range(size), key=lambda t, z=z: (abs(t - z), t)) for z in range(size)]


def shifted(size, source, dest, c):
    to_end = ((dest == 0) | (dest == size - 1)) & (c >= CHUNKS - END_SHIFT)
    from_end = (source == 0) | (source == size - 1)
    return to_end | from_end


def fused_kernel(
    counts,
    adapters,
    pool_rows,
    tokens,
    weight,
    down,
    up,
    xg,
    out,
    acc,
    xv,
    wbuf,
    d0,
    d1,
    d_pick,
    d_all,
    d_relay,
    u1,
    u_pick,
    u_all,
    u_relay,
    part,
    s_in,
    s_mid,
    s_row,
    shrunk,
    stage,
    recv,
    up_sem,
    dn_sem,
    y_sem,
    x_sem,
    w_sem,
    d0_sem,
    d1_sem,
    d2_sem,
    dr_sem,
    u1_sem,
    u2_sem,
    ur_sem,
    s_sem,
    row_sem,
    g_sem,
    o_sem,
):
    groups = lax.axis_size("grp")
    size, cores = lax.axis_size("tp"), lax.axis_size("cores")
    n = size * cores
    g, z, y = lax.axis_index("grp"), lax.axis_index("tp"), lax.axis_index("cores")
    me = z * cores + y
    other = 1 - y
    token_count, depth = tokens.shape
    rows = token_count // CHUNKS
    hidden = weight.shape[2]
    cols = wbuf.shape[-1]
    blocks = hidden // cols
    per = n // groups
    share = token_count // n
    order = reach(size)
    seg_count = adapters.shape[1]
    rank = up.shape[1]
    narrow = up.shape[2] // 2

    ends = []
    for k in range(seg_count):
        ends.append(counts[0, k] + (ends[-1] if ends else 0))
    tile_seg = []
    for t in range(token_count // TILE):
        seg = 0
        for k in range(seg_count - 1):
            seg = seg + jnp.where(ends[k] <= t, 1, 0)
        tile_seg.append(seg)

    def peer(k):
        return {"grp": lax.rem(g + k, groups)}

    def span(c):
        if isinstance(c, int):
            return pl.ds(c * rows, rows)
        return pl.ds(pl.multiple_of(c * rows, rows), rows)

    def remote(src, dst, send, receive, dev):
        return pltpu.make_async_remote_copy(
            src_ref=src,
            dst_ref=dst,
            send_sem=send,
            recv_sem=receive,
            device_id=dev,
            device_id_type=MESH,
        )


    def hop(src, s, c, sems, dev):
        return remote(src, xg.at[s, span(c)], sems.at[s, c], recv.at[s, c], dev)

    up_dev, dn_dev, y_dev = {"tp": z + 1}, {"tp": z - 1}, {"cores": other}

    def arrived(s, c):
        hop(xg.at[s, span(c)], s, c, y_sem, y_dev).wait_recv()

    def forward(s, c, sems, dev):
        hop(xg.at[s, span(c)], s, c, sems, dev).start()

    def send_own(c):
        src = tokens.at[span(c)]

        @pl.when(z + 1 < size)
        def _():
            hop(src, me, c, up_sem, up_dev).start()

        @pl.when(z >= 1)
        def _():
            hop(src, me, c, dn_sem, dn_dev).start()

        hop(src, me, c, y_sem, y_dev).start()

    def row_arrival(r, c, first):
        lo, hi = z - r, z + r

        @pl.when(lo >= 0)
        def _():
            s = lo * cores + y
            arrived(s, c)

            @pl.when(z + 1 < size)
            def _():
                forward(s, c, up_sem, up_dev)

            @pl.when(jnp.logical_not(shifted(size, lo, z, c)) if first else z >= 0)
            def _():
                forward(s, c, y_sem, y_dev)

        @pl.when(hi < size)
        def _():
            s = hi * cores + y
            arrived(s, c)

            @pl.when(z >= 1)
            def _():
                forward(s, c, dn_sem, dn_dev)

            @pl.when(jnp.logical_not(shifted(size, hi, z, c)) if first else z >= 0)
            def _():
                forward(s, c, y_sem, y_dev)

    def mate_arrival(c):
        s = z * cores + other
        arrived(s, c)

        @pl.when((z + 1 < size) & shifted(size, z, z + 1, c))
        def _():
            forward(s, c, up_sem, up_dev)

        @pl.when((z >= 1) & shifted(size, z, z - 1, c))
        def _():
            forward(s, c, dn_sem, dn_dev)


    def w_copy(piece, j, slot, k):
        return pltpu.make_async_copy(
            weight.at[
                pl.ds(pl.multiple_of(piece * depth, depth), depth),
                slice(None),
                pl.ds(pl.multiple_of(j * cols, cols), cols),
            ],
            wbuf.at[slot, k],
            w_sem.at[slot, k],
        )

    def first_tiles(pieces):
        for k, piece in enumerate(pieces):
            w_copy(piece, 0, 0, k).start()

    def x_copy(src, k):
        return pltpu.make_async_copy(src, xv.at[k], x_sem.at[k])

    def tile_product(pieces, slots, j, where, first):
        slot = lax.rem(j, 2)

        @pl.when(j + 1 < blocks)
        def _():
            for k, piece in enumerate(pieces):
                w_copy(piece, j + 1, 1 - slot, k).start()

        at = pl.ds(pl.multiple_of(j * cols, cols), cols)
        for k, piece in enumerate(pieces):
            w_copy(piece, j, slot, k).wait()
        ws = [jnp.swapaxes(wbuf[slot, k], 0, 1) for k in range(len(pieces))]
        totals = []
        for h in range(2):
            total = None if first else acc[h, where, at]
            for k, x in enumerate(slots):
                term = jnp.dot(xv[x, where], ws[k][h], preferred_element_type=jnp.float32)
                total = term if total is None else total + term
            totals.append(total)
        return at, totals

    def multiply(pieces, slots, j, first):
        at, totals = tile_product(pieces, slots, j, pl.ds(0, token_count), first)
        for h in range(2):
            acc[h, :, at] = totals[h]


    near_end = (z == 1) | (z == size - 2)
    end = jnp.where(z == 1, 0, size - 1)

    def relayed(p_z, p_y, s_z, s_y):
        return ((p_z == 0) | (p_z == size - 1)) & (p_y != s_y) & (p_z != s_z)

    def relay_dev(p_z, p_y):
        return {"tp": jnp.where(p_z == 0, 1, size - 2), "cores": p_y}

    def scatter(source, final, relay, sems, relay_sems, act):
        for k in range(1, n):
            p = lax.rem(me + k, n)
            p_z, p_y = p // cores, lax.rem(p, cores)
            far = relayed(p_z, p_y, z, y)

            @pl.when(far)
            def _():
                copy = remote(
                    source(p), relay.at[z], sems.at[0, p], relay_sems.at[0, z],
                    relay_dev(p_z, p_y),
                )
                act(copy)

            @pl.when(jnp.logical_not(far))
            def _():
                copy = remote(
                    source(p), final.at[me], sems.at[0, p], sems.at[1, me],
                    {"tp": p_z, "cores": p_y},
                )
                act(copy)

    def relay_copy(final, relay, sems, relay_sems, k):
        s_z = lax.rem(end + k, size)
        s = s_z * cores + other
        return s_z, remote(
            relay.at[s_z], final.at[s], relay_sems.at[1, s_z], sems.at[1, s], {"tp": end}
        )

    def pass_on(final, relay, sems, relay_sems):
        @pl.when(near_end)
        def _():
            for k in range(1, size):
                s_z, copy = relay_copy(final, relay, sems, relay_sems, k)
                remote(
                    relay.at[s_z], relay.at[s_z], relay_sems.at[1, s_z], relay_sems.at[0, s_z],
                    {"tp": end},
                ).wait_recv()
                copy.start()

    def scattered(final, sems):
        for k in range(1, n):
            s = lax.rem(me + k, n)
            remote(final.at[s], final.at[s], sems.at[0, s], sems.at[1, s], y_dev).wait_recv()

    def relays_done(final, relay, sems, relay_sems):
        @pl.when(near_end)
        def _():
            for k in range(1, size):
                relay_copy(final, relay, sems, relay_sems, k)[1].wait_send()

    def started(copy):
        copy.start()

    def sent(copy):
        copy.wait_send()

    def d_source(p):
        return d0.at[p // per, lax.rem(p, per)]

    def u_source(p):
        return up.at[p]

    def d_scatter(act):
        scatter(d_source, d1, d_relay, d1_sem, dr_sem, act)

    def u_scatter(act):
        scatter(u_source, u1, u_relay, u1_sem, ur_sem, act)

    def d0_copy(k):
        return remote(
            down.at[:, lax.rem(g + k, groups)], d0.at[g], d0_sem.at[0, k], d0_sem.at[1, k], peer(k)
        )

    def d2_copy(k):
        return remote(d_pick.at[k], d_all.at[g], d2_sem.at[0, k], d2_sem.at[1, k], peer(k))

    def u2_copy(k):
        return remote(u_pick.at[k], u_all.at[g], u2_sem.at[0, k], u2_sem.at[1, k], peer(k))

    def pick(source, picked, mine):
        for k in range(groups):
            which = lax.rem(g + k, groups)
            for j in range(seg_count):
                value = source[pool_rows[adapters[which, j]]]
                if k:
                    picked[k, j] = value
                else:
                    mine[g, j] = value


    def sy_copy():
        return remote(part.at[:, other], s_in, s_sem.at[0], s_sem.at[1], y_dev)

    def sz_copy(k):
        p = lax.rem(z + k, size)
        return remote(s_mid.at[p], s_row.at[k], row_sem.at[0, k], row_sem.at[1, k], {"tp": p})

    def gz_copy(k):
        p = lax.rem(z + k, size)
        return remote(
            shrunk.at[z, y], shrunk.at[z, y], g_sem.at[0, k], g_sem.at[1, k], {"tp": p}
        )

    def gy_copy():
        return remote(shrunk.at[:, y], shrunk.at[:, y], s_sem.at[2], s_sem.at[3], y_dev)

    def shrink():
        piece = depth // groups
        for t in range(token_count // TILE):
            at = slice(t * TILE, (t + 1) * TILE)
            total = None
            for j in range(groups):
                term = jnp.dot(
                    xv[2, at, j * piece : (j + 1) * piece],
                    d_all[j, tile_seg[t]],
                    preferred_element_type=jnp.float32,
                )
                total = term if total is None else total + term
            for i in range(max(1, TILE // share)):
                p = (t * TILE) // share + i
                low = (t * TILE) % share
                length = min(share, TILE)
                part[p // cores, p % cores, low : low + length] = total[
                    i * length : (i + 1) * length
                ]

    def here(src, dst, k):
        return pltpu.make_async_copy(src, dst, o_sem.at[k])


    for k in range(1, groups):
        d0_copy(k).start()
    here(down.at[:, g], d0.at[g], 0).start()
    x_copy(tokens, 2).start()
    first_tiles([me])
    send_own(0)
    here(up.at[me], u1.at[me], 2).start()
    here(down.at[:, g], d0.at[g], 0).wait()
    for k in range(1, groups):
        d0_copy(k).wait_recv()
    d_scatter(started)
    here(d0.at[me // per, lax.rem(me, per)], d1.at[me], 1).start()
    for c in range(1, CHUNKS):
        send_own(c)
    u_scatter(started)
    x_copy(tokens, 2).wait()

    step = blocks // CHUNKS

    def own_tiles(c):
        def one(i, carry):
            multiply([me], [2], c * step + i, True)
            return carry

        lax.fori_loop(0, step, one, 0)

    for c in range(CHUNKS):
        row_arrival(1, c, True)
        mate_arrival(c)
        if c == 1:
            pass_on(d1, d_relay, d1_sem, dr_sem)
        if c == CHUNKS - 1:
            here(d0.at[me // per, lax.rem(me, per)], d1.at[me], 1).wait()
            scattered(d1, d1_sem)
            pick(d1, d_pick, d_all)
            pass_on(u1, u_relay, u1_sem, ur_sem)
            for k in range(1, groups):
                d2_copy(k).start()
        own_tiles(c)

    def later_round(r, carry):
        pieces = [
            table(order, z, r - 1) * cores + y,
            table(order, z, r - 2) * cores + other,
        ]

        @pl.when(r >= 3)
        def _():
            for c in range(CHUNKS):
                arrived(pieces[1], c)

        for k in range(2):
            x_copy(xg.at[pieces[k]], k).start()
        first_tiles(pieces)
        for k in range(2):
            x_copy(xg.at[pieces[k]], k).wait()

        def body(c, carry):
            @pl.when(r < size)
            def _():
                row_arrival(r, c, False)

            @pl.when((r == 2) & (c == 0))
            def _():
                for k in range(1, groups):
                    d2_copy(k).wait_recv()
                shrink()
                here(up.at[me], u1.at[me], 2).wait()
                scattered(u1, u1_sem)
                pick(u1, u_pick, u_all)
                sy_copy().start()

            @pl.when((r == 2) & (c == 1))
            def _():
                for k in range(1, groups):
                    u2_copy(k).start()

            @pl.when((r == 2) & (c == 2))
            def _():
                sy_copy().wait_recv()
                for k in range(size):
                    s_mid[k] = part[k, y] + s_in[k]

            @pl.when((r == 2) & (c == 3))
            def _():
                for k in range(1, size):
                    sz_copy(k).start()

            @pl.when((r == 3) & (c == 0))
            def _():
                mine = s_mid[z]
                for k in range(1, size):
                    sz_copy(k).wait_recv()
                    mine = mine + s_row[k]
                shrunk[z, y] = mine.astype(shrunk.dtype)

            @pl.when((r == 3) & (c == 1))
            def _():
                for k in range(1, size):
                    gz_copy(k).start()

            @pl.when((r == 3) & (c == 2))
            def _():
                for k in range(1, size):
                    p = lax.rem(z + size - k, size)
                    remote(
                        shrunk.at[p, y], shrunk.at[p, y], g_sem.at[0, k], g_sem.at[1, k], y_dev
                    ).wait_recv()
                gy_copy().start()

            def one(i, carry):
                multiply(pieces, [0, 1], c * step + i, False)
                return carry

            lax.fori_loop(0, step, one, 0)
            return carry

        lax.fori_loop(0, CHUNKS, body, 0)
        return carry

    lax.fori_loop(2, size + 1, later_round, 0)


    last = table(order, z, size - 1) * cores + other

    def last_x(c):
        return pltpu.make_async_copy(xg.at[last, span(c)], xv.at[0, span(c)], x_sem.at[0])

    def stage_copy(c):
        return pltpu.make_async_copy(stage.at[c % 2], out.at[span(c)], o_sem.at[4 + c % 2])

    def tail(c):
        def one(j, carry):
            at, totals = tile_product([last], [0], j, span(c), False)
            m = (j * cols) // narrow
            low = lax.rem(j * cols, narrow)
            for t in range(rows // TILE):
                tile = c * (rows // TILE) + t
                both = []
                for h in range(2):
                    parts = []
                    for i in range(max(1, TILE // share)):
                        p = (tile * TILE) // share + i
                        first = (tile * TILE) % share
                        parts.append(
                            shrunk[
                                p // cores,
                                p % cores,
                                first : first + min(share, TILE),
                                h * rank : (h + 1) * rank,
                            ]
                        )
                    x = parts[0] if len(parts) == 1 else jnp.concatenate(parts, 0)
                    delta = jnp.dot(
                        x,
                        u_all[
                            m,
                            tile_seg[tile],
                            :,
                            pl.ds(pl.multiple_of(h * narrow + low, cols), cols),
                        ],
                        preferred_element_type=jnp.float32,
                    )
                    both.append(
                        totals[h][t * TILE : (t + 1) * TILE] + adapter_scale * delta
                    )
                gate, lift = both
                value = gate / (1.0 + jnp.exp(-gate)) * lift
                stage[c % 2, t * TILE : (t + 1) * TILE, at] = value.astype(stage.dtype)
            return carry

        lax.fori_loop(0, blocks, one, 0)

    def drain(i, carry):
        t, c = i // CHUNKS, lax.rem(i, CHUNKS)
        s, across = t * cores + y, t * cores + other

        def done(s, sems, dev):
            hop(xg.at[s, span(c)], s, c, sems, dev).wait_send()

        @pl.when((z + 1 < size) & (t <= z))
        def _():
            done(s, up_sem, up_dev)

        @pl.when((z >= 1) & (t >= z))
        def _():
            done(s, dn_sem, dn_dev)

        near = (t == z - 1) | (t == z + 1)

        @pl.when(jnp.logical_not(near & shifted(size, t, z, c)))
        def _():
            done(s, y_sem, y_dev)

        @pl.when((t == z) & (z + 1 < size) & shifted(size, z, z + 1, c))
        def _():
            done(across, up_sem, up_dev)

        @pl.when((t == z) & (z >= 1) & shifted(size, z, z - 1, c))
        def _():
            done(across, dn_sem, dn_dev)

        return carry

    def all_sent():
        for k in range(1, groups):
            d0_copy(k).wait_send()
            d2_copy(k).wait_send()
            u2_copy(k).wait_send()
        d_scatter(sent)
        u_scatter(sent)
        relays_done(d1, d_relay, d1_sem, dr_sem)
        relays_done(u1, u_relay, u1_sem, ur_sem)
        sy_copy().wait_send()
        gy_copy().wait_send()
        for k in range(1, size):
            sz_copy(k).wait_send()
            gz_copy(k).wait_send()
        lax.fori_loop(0, size * CHUNKS, drain, 0)

    for c in range(CHUNKS):
        first_tiles([last])
        if c == 0:
            for k in range(1, groups):
                u2_copy(k).wait_recv()
            remote(
                shrunk.at[:, other], shrunk.at[:, other], s_sem.at[2], s_sem.at[3], y_dev
            ).wait_recv()
        if c == CHUNKS - 1:
            all_sent()
        arrived(last, c)
        last_x(c).start()
        if c >= 2:
            stage_copy(c - 2).wait()
        last_x(c).wait()
        tail(c)
        stage_copy(c).start()
    for c in range(max(0, CHUNKS - 2), CHUNKS):
        stage_copy(c).wait()


def fused_call(counts, adapters, pool_rows, tokens, weight, down, up, groups, size, cores):
    n = size * cores
    token_count, depth = tokens.shape
    hidden = weight.shape[2]
    cols = min(BLOCK_COLS, hidden)
    twice_rank = down.shape[-1]
    share = token_count // n
    segs = adapters.shape[1]
    dma = pltpu.SemaphoreType.DMA
    any_space = pl.BlockSpec(memory_space=pl.ANY)
    smem = pl.BlockSpec(memory_space=pltpu.SMEM)
    block = down.shape[2:]
    leaf = up.shape[1:]
    vmem = pltpu.VMEM
    return pl.pallas_call(
        fused_kernel,
        out_shape=(
            jax.ShapeDtypeStruct((n, token_count, depth), tokens.dtype),
            jax.ShapeDtypeStruct((token_count, hidden), jnp.bfloat16),
        ),
        in_specs=[smem] * 3 + [any_space] * 4,
        out_specs=(any_space,) * 2,
        scratch_shapes=[
            vmem((2, token_count, hidden), jnp.float32),
            vmem((3, token_count, depth), tokens.dtype),
            vmem((2, 2, depth, 2, cols), weight.dtype),
            vmem((groups, n // groups) + block, down.dtype),
            vmem((n,) + block, down.dtype),
            vmem((groups, segs) + block, down.dtype),
            vmem((groups, segs) + block, down.dtype),
            vmem((size,) + block, down.dtype),
            vmem((n,) + leaf, up.dtype),
            vmem((groups, segs) + leaf, up.dtype),
            vmem((groups, segs) + leaf, up.dtype),
            vmem((size,) + leaf, up.dtype),
            vmem((size, cores, share, twice_rank), jnp.float32),
            vmem((size, share, twice_rank), jnp.float32),
            vmem((size, share, twice_rank), jnp.float32),
            vmem((size, share, twice_rank), jnp.float32),
            vmem((size, cores, share, twice_rank), jnp.bfloat16),
            vmem((2, token_count // CHUNKS, hidden), jnp.bfloat16),
            dma((n, CHUNKS)),
            dma((n, CHUNKS)),
            dma((n, CHUNKS)),
            dma((n, CHUNKS)),
            dma((3,)),
            dma((2, 2)),
            dma((2, groups)),
            dma((2, n)),
            dma((2, groups)),
            dma((2, size)),
            dma((2, n)),
            dma((2, groups)),
            dma((2, size)),
            dma((4,)),
            dma((2, size)),
            dma((2, size)),
            dma((6,)),
        ],
        compiler_params=pltpu.CompilerParams(
            vmem_limit_bytes=VMEM_LIMIT, has_side_effects=True
        ),
        name="fused",
    )(counts, adapters, pool_rows, tokens, weight, down, up)


def compute_fused(
    tokens,
    gate_up_weight,
    down_factor_pool,
    up_factor_pool,
    segment_adapters,
    segment_tile_counts,
    adapter_pool_rows,
):
    groups = lax.axis_size("grp")
    size, cores = lax.axis_size("tp"), lax.axis_size("cores")
    n = size * cores
    depth = tokens.shape[1]
    down = down_factor_pool.reshape(
        n // groups, groups, depth // groups, down_factor_pool.shape[2]
    )
    up = up_factor_pool.reshape(up_factor_pool.shape[2:])
    return fused_call(
        segment_tile_counts,
        segment_adapters,
        adapter_pool_rows,
        tokens,
        gate_up_weight,
        down,
        up,
        groups,
        size,
        cores,
    )[1]


def fits(mesh):
    size, cores, groups = mesh.shape["tp"], mesh.shape["cores"], mesh.shape["grp"]
    return cores == 2 and size == groups and (size * cores) % groups == 0 and size == 4


def per_device(*args):
    return compute(*args)


def compute(
    tokens,
    gate_up_weight,
    down_factor_pool,
    up_factor_pool,
    segment_adapters,
    segment_tile_counts,
    adapter_pool_rows,
):
    groups = lax.axis_size("grp")
    tp_size, cores_size = lax.axis_size("tp"), lax.axis_size("cores")
    n = tp_size * cores_size
    token_count, depth = tokens.shape
    local_hidden_width = gate_up_weight.shape[2]
    twice_rank = down_factor_pool.shape[2]
    narrow = local_hidden_width // groups
    seg_count = segment_adapters.shape[1]
    half = token_count // 2

    me = ring_position(lax.axis_index("tp"), lax.axis_index("cores"), tp_size)
    order = [ring_device(k, tp_size, cores_size) for k in range(n)]
    forward = [(order[k], order[(k + 1) % n]) for k in range(n)]
    backward = [(order[(k + 1) % n], order[k]) for k in range(n)]

    def owner(shift):
        return ring_device((me + shift + n) % n, tp_size, cores_size).astype(jnp.int32)

    full_steps = (n - 1) // 2
    lefts, rights = [tokens], [tokens]
    for _ in range(1, full_steps + 1):
        lefts.append(lax.ppermute(lefts[-1], TP, forward))
        rights.append(lax.ppermute(rights[-1], TP, backward))
    last_top = lax.ppermute(lefts[-1][:half], TP, forward)
    last_bottom = lax.ppermute(rights[-1][half:], TP, backward)

    piece = depth // groups
    a = down_factor_pool.reshape(n // groups, groups, piece, twice_rank)
    a = lax.all_to_all(a, "grp", split_axis=1, concat_axis=0, tiled=True)
    a = a.reshape(n, piece, twice_rank)
    a = lax.all_to_all(a, TP, split_axis=0, concat_axis=0, tiled=True)
    b = up_factor_pool.reshape(up_factor_pool.shape[2:])
    b = lax.all_to_all(b, TP, split_axis=0, concat_axis=0, tiled=True)
    slots = jnp.take(adapter_pool_rows, segment_adapters, mode="clip")
    a = group_exchange(a, slots)
    b = group_exchange(b, slots)
    block_cols = narrow
    if narrow % 128:
        block_cols = local_hidden_width
        b = b.reshape(groups, seg_count, b.shape[2], 2, narrow)
        b = jnp.transpose(b, (1, 2, 3, 0, 4))
        b = b.reshape(1, seg_count, b.shape[1], 2 * block_cols)

    tile_count = token_count // TILE
    tile_seg = tile_segments(segment_tile_counts[0], tile_count).astype(jnp.int32)
    row_seg = jnp.repeat(tile_seg, TILE)[:, None]
    partial = None
    for j in range(seg_count):
        term = jnp.dot(
            tokens, a[:, j].reshape(depth, twice_rank), preferred_element_type=jnp.float32
        )
        partial = term if partial is None else jnp.where(row_seg == j, term, partial)
    share = token_count // n
    partial = lax.all_to_all(
        partial.reshape(n, share, twice_rank), TP, split_axis=0, concat_axis=0, tiled=True
    )
    own = jnp.sum(partial, axis=0).astype(jnp.bfloat16)
    shrunk = lax.all_to_all(
        jnp.broadcast_to(own[None], (n, share, twice_rank)),
        TP,
        split_axis=0,
        concat_axis=0,
        tiled=True,
    ).reshape(token_count, twice_rank)

    acc = None
    for s in range(1, full_steps + 1):
        xs = [lefts[s], rights[s]]
        rows = [owner(-s), owner(s)]
        if s == 1:
            xs.insert(0, tokens)
            rows.insert(0, owner(0))
        acc = partial_matmul(xs, gate_up_weight, jnp.stack(rows), acc, block_cols)
    return final_matmul(
        last_top, last_bottom, gate_up_weight, jnp.stack([owner(n // 2)]), acc, shrunk, b, tile_seg
    )


def fused(*args):
    return compute_fused(*args)


def solution(mesh):
    direct = fits(mesh)
    return jax.shard_map(
        fused if direct else per_device,
        mesh=mesh,
        in_specs=(
            P("grp", ("tp", "cores")),
            P(None, None, ("tp", "cores")),
            P(("tp", "cores"), "grp", None),
            P(("tp", "cores"), "grp", None, None, None),
            P(),
            P("grp", None),
            P(),
        ),
        out_specs=P("grp", ("tp", "cores")),
        check_vma=False,
    )
```

```python
import functools

import jax
import jax.numpy as jnp
from jax import lax
from jax.experimental import pallas as pl
from jax.experimental.pallas import tpu as pltpu
from jax.sharding import PartitionSpec as P


TILE = 128
VMEM_LIMIT = 60 * 1024 * 1024

adapter_scale = 0.5


TP = ("tp", "cores")


def tile_segments(tile_lengths, tile_count):
    bounds = jnp.cumsum(tile_lengths)
    positions = jnp.arange(tile_count, dtype=jnp.int32)
    return jnp.sum((bounds[None, :] <= positions[:, None]).astype(jnp.int32), axis=1)


def ring_device(position, tp_size, cores_size):
    c = position // tp_size
    t = position % tp_size
    t = t + (c % 2) * (tp_size - 1 - 2 * t)
    return t * cores_size + c


def ring_position(tp_index, cores_index, tp_size):
    t = tp_index + (cores_index % 2) * (tp_size - 1 - 2 * tp_index)
    return cores_index * tp_size + t


def partial_kernel(count, with_acc, rows_ref, *refs):
    xs, ws = refs[:count], refs[count : 2 * count]
    out = refs[-1]
    ws = [jnp.swapaxes(w[...], 0, 1) for w in ws]
    for h in range(2):
        total = refs[2 * count][h] if with_acc else None
        for x, w in zip(xs, ws):
            term = jnp.dot(x[...], w[h], preferred_element_type=jnp.float32)
            total = term if total is None else total + term
        out[h] = total


def partial_matmul(xs, weight, rows, acc, block_cols):
    count = len(xs)
    tokens, depth = xs[0].shape
    hidden = weight.shape[2]
    block_cols = min(block_cols, 256)
    in_specs = [pl.BlockSpec((tokens, depth), lambda j, r: (0, 0))] * count
    for k in range(count):
        in_specs.append(
            pl.BlockSpec((depth, 2, block_cols), lambda j, r, k=k: (r[k], 0, j))
        )
    acc_spec = pl.BlockSpec((2, tokens, block_cols), lambda j, r: (0, 0, j))
    operands = list(xs) + [weight] * count
    aliases = {}
    if acc is not None:
        in_specs.append(acc_spec)
        aliases = {1 + len(operands): 0}
        operands.append(acc)
    return pl.pallas_call(
        functools.partial(partial_kernel, count, acc is not None),
        out_shape=jax.ShapeDtypeStruct((2, tokens, hidden), jnp.float32),
        grid_spec=pltpu.PrefetchScalarGridSpec(
            num_scalar_prefetch=1,
            grid=(hidden // block_cols,),
            in_specs=in_specs,
            out_specs=acc_spec,
        ),
        input_output_aliases=aliases,
        compiler_params=pltpu.CompilerParams(vmem_limit_bytes=VMEM_LIMIT),
        cost_estimate=pl.CostEstimate(
            flops=4 * count * tokens * depth * hidden,
            bytes_accessed=count * 4 * depth * hidden + 16 * tokens * hidden,
            transcendentals=0,
        ),
    )(rows, *operands)


def final_kernel(tiles_per_half, rank, rows_ref, seg_ref, xt, xb, w, acc, shrunk, b, out, total):
    narrow = out.shape[1]
    w = jnp.swapaxes(w[...], 0, 1)
    for p, x in enumerate((xt, xb)):
        for h in range(2):
            span = slice(p * x.shape[0], (p + 1) * x.shape[0])
            total[h, span] = acc[h, span] + jnp.dot(
                x[...], w[h], preferred_element_type=jnp.float32
            )
        for t in range(p * tiles_per_half, (p + 1) * tiles_per_half):
            seg = seg_ref[t]
            span = slice(t * TILE, (t + 1) * TILE)
            both = []
            for h in range(2):
                delta = jnp.dot(
                    shrunk[span, h * rank : (h + 1) * rank],
                    b[0, seg, :, h * narrow : (h + 1) * narrow],
                    preferred_element_type=jnp.float32,
                )
                both.append(total[h, span] + adapter_scale * delta)
            gate, up = both
            out[span] = (gate / (1.0 + jnp.exp(-gate)) * up).astype(out.dtype)


def final_matmul(xt, xb, weight, rows, acc, shrunk, b_chosen, tile_seg):
    half, depth = xt.shape
    tokens = 2 * half
    hidden = weight.shape[2]
    blocks, segs, rank, twice = b_chosen.shape
    narrow = twice // 2
    return pl.pallas_call(
        functools.partial(final_kernel, half // TILE, rank),
        out_shape=jax.ShapeDtypeStruct((tokens, hidden), jnp.bfloat16),
        grid_spec=pltpu.PrefetchScalarGridSpec(
            num_scalar_prefetch=2,
            grid=(blocks,),
            in_specs=[
                pl.BlockSpec((half, depth), lambda j, r, s: (0, 0)),
                pl.BlockSpec((half, depth), lambda j, r, s: (0, 0)),
                pl.BlockSpec((depth, 2, narrow), lambda j, r, s: (r[0], 0, j)),
                pl.BlockSpec((2, tokens, narrow), lambda j, r, s: (0, 0, j)),
                pl.BlockSpec((tokens, 2 * rank), lambda j, r, s: (0, 0)),
                pl.BlockSpec((1, segs, rank, twice), lambda j, r, s: (j, 0, 0, 0)),
            ],
            out_specs=pl.BlockSpec((tokens, narrow), lambda j, r, s: (0, j)),
            scratch_shapes=[pltpu.VMEM((2, tokens, narrow), jnp.float32)],
        ),
        compiler_params=pltpu.CompilerParams(vmem_limit_bytes=VMEM_LIMIT),
        cost_estimate=pl.CostEstimate(
            flops=4 * tokens * (depth + rank) * hidden,
            bytes_accessed=4 * depth * hidden + 10 * tokens * hidden,
            transcendentals=tokens * hidden,
        ),
    )(rows, tile_seg, xt, xb, weight, acc, shrunk, b_chosen)


def group_exchange(pool, slots):
    groups = lax.axis_size("grp")
    g = lax.axis_index("grp")
    parts = []
    for k in range(groups):
        wanted = lax.dynamic_index_in_dim(slots, (g + k) % groups, 0, keepdims=False)
        part = jnp.take(pool, wanted, axis=0, mode="clip")
        if k:
            pairs = [(i, (i + k) % groups) for i in range(groups)]
            part = lax.ppermute(part, "grp", pairs)
        parts.append(part)
    sources = (g + groups - jnp.arange(groups)) % groups
    return jnp.take(jnp.stack(parts), sources, axis=0, mode="clip")


MESH = pl.DeviceIdType.MESH
CHUNKS = 4
END_SHIFT = 0
BLOCK_COLS = 256


def table(rows, i, k):
    total = 0
    for a, row in enumerate(rows):
        for b, value in enumerate(row):
            if value:
                total = total + jnp.where((i == a) & (k == b), value, 0)
    return total


def reach(size):
    return [sorted(range(size), key=lambda t, z=z: (abs(t - z), t)) for z in range(size)]


def shifted(size, source, dest, c):
    to_end = ((dest == 0) | (dest == size - 1)) & (c >= CHUNKS - END_SHIFT)
    from_end = (source == 0) | (source == size - 1)
    return to_end | from_end


def fused_kernel(
    counts,
    adapters,
    pool_rows,
    tokens,
    weight,
    down,
    up,
    xg,
    out,
    acc,
    xv,
    wbuf,
    d_all,
    low,
    u1,
    u_pick,
    u_all,
    u_relay,
    part,
    s_in,
    shrunk,
    stage,
    recv,
    up_sem,
    dn_sem,
    y_sem,
    x_sem,
    w_sem,
    d_sem,
    u1_sem,
    u2_sem,
    ur_sem,
    s_sem,
    g_sem,
    o_sem,
):
    groups = lax.axis_size("grp")
    size, cores = lax.axis_size("tp"), lax.axis_size("cores")
    n = size * cores
    g, z, y = lax.axis_index("grp"), lax.axis_index("tp"), lax.axis_index("cores")
    me = z * cores + y
    other = 1 - y
    token_count, depth = tokens.shape
    rows = token_count // CHUNKS
    hidden = weight.shape[2]
    cols = wbuf.shape[-1]
    blocks = hidden // cols
    per = n // groups
    order = reach(size)
    seg_count = adapters.shape[1]
    rank = up.shape[1]
    narrow = up.shape[2] // 2
    piece_rows = rows // n

    ends = []
    for k in range(seg_count):
        ends.append(counts[0, k] + (ends[-1] if ends else 0))
    tile_seg = []
    for t in range(token_count // TILE):
        seg = 0
        for k in range(seg_count - 1):
            seg = seg + jnp.where(ends[k] <= t, 1, 0)
        tile_seg.append(seg)

    def peer(k):
        return {"grp": lax.rem(g + k, groups)}

    def span(c):
        if isinstance(c, int):
            return pl.ds(c * rows, rows)
        return pl.ds(pl.multiple_of(c * rows, rows), rows)

    def remote(src, dst, send, receive, dev):
        return pltpu.make_async_remote_copy(
            src_ref=src,
            dst_ref=dst,
            send_sem=send,
            recv_sem=receive,
            device_id=dev,
            device_id_type=MESH,
        )


    def hop(src, s, c, sems, dev):
        return remote(src, xg.at[s, span(c)], sems.at[s, c], recv.at[s, c], dev)

    up_dev, dn_dev, y_dev = {"tp": z + 1}, {"tp": z - 1}, {"cores": other}

    def arrived(s, c):
        hop(xg.at[s, span(c)], s, c, y_sem, y_dev).wait_recv()

    def forward(s, c, sems, dev):
        hop(xg.at[s, span(c)], s, c, sems, dev).start()

    def send_row(c):
        src = tokens.at[span(c)]

        @pl.when(z + 1 < size)
        def _():
            hop(src, me, c, up_sem, up_dev).start()

        @pl.when(z >= 1)
        def _():
            hop(src, me, c, dn_sem, dn_dev).start()

    def send_mate(c):
        hop(tokens.at[span(c)], me, c, y_sem, y_dev).start()

    def row_arrival(r, c, first):
        lo, hi = z - r, z + r

        @pl.when(lo >= 0)
        def _():
            s = lo * cores + y
            arrived(s, c)

            @pl.when(z + 1 < size)
            def _():
                forward(s, c, up_sem, up_dev)

            @pl.when(jnp.logical_not(shifted(size, lo, z, c)) if first else z >= 0)
            def _():
                forward(s, c, y_sem, y_dev)

        @pl.when(hi < size)
        def _():
            s = hi * cores + y
            arrived(s, c)

            @pl.when(z >= 1)
            def _():
                forward(s, c, dn_sem, dn_dev)

            @pl.when(jnp.logical_not(shifted(size, hi, z, c)) if first else z >= 0)
            def _():
                forward(s, c, y_sem, y_dev)

    def mate_arrival(c):
        s = z * cores + other
        arrived(s, c)

        @pl.when((z + 1 < size) & shifted(size, z, z + 1, c))
        def _():
            forward(s, c, up_sem, up_dev)

        @pl.when((z >= 1) & shifted(size, z, z - 1, c))
        def _():
            forward(s, c, dn_sem, dn_dev)


    def w_copy(piece, j, slot, k):
        return pltpu.make_async_copy(
            weight.at[
                pl.ds(pl.multiple_of(piece * depth, depth), depth),
                slice(None),
                pl.ds(pl.multiple_of(j * cols, cols), cols),
            ],
            wbuf.at[slot, k],
            w_sem.at[slot, k],
        )

    def first_tiles(pieces):
        for k, piece in enumerate(pieces):
            w_copy(piece, 0, 0, k).start()

    def x_copy(src, k):
        return pltpu.make_async_copy(src, xv.at[k], x_sem.at[k])

    def multiply(pieces, j, low_row, count, first):
        slot = lax.rem(j, 2)

        @pl.when(j + 1 < blocks)
        def _():
            for k, piece in enumerate(pieces):
                w_copy(piece, j + 1, 1 - slot, k).start()

        at = pl.ds(pl.multiple_of(j * cols, cols), cols)
        where = pl.ds(low_row, count)
        for k, piece in enumerate(pieces):
            w_copy(piece, j, slot, k).wait()
        ws = [jnp.swapaxes(wbuf[slot, k], 0, 1) for k in range(len(pieces))]
        for h in range(2):
            total = None if first else acc[h, where, at]
            for k in range(len(pieces)):
                term = jnp.dot(xv[k, where], ws[k][h], preferred_element_type=jnp.float32)
                total = term if total is None else total + term
            acc[h, where, at] = total

    def run_round(pieces, sources, first=False, project=True, hooks=()):
        first_tiles(pieces)
        copies = [x_copy(src, k) for k, src in enumerate(sources)]
        for copy in copies:
            copy.start()
        for copy in copies:
            copy.wait()
        if project:
            for k, piece in enumerate(pieces):
                low[...] = low[...] + jnp.dot(
                    xv[k], d_all[piece], preferred_element_type=jnp.float32
                )

        def one(j, carry):
            multiply(pieces, j, 0, token_count, first)
            for i, hook in enumerate(hooks):
                pl.when(j == (i + 1) * blocks // len(hooks) - 1)(hook)
            return carry

        lax.fori_loop(0, blocks, one, 0)


    near_end = (z == 1) | (z == size - 2)
    end = jnp.where(z == 1, 0, size - 1)

    def relayed(p_z, p_y, s_z, s_y):
        return ((p_z == 0) | (p_z == size - 1)) & (p_y != s_y) & (p_z != s_z)

    def relay_dev(p_z, p_y):
        return {"tp": jnp.where(p_z == 0, 1, size - 2), "cores": p_y}

    def scatter(source, final, relay, sems, relay_sems, act):
        for k in range(1, n):
            p = lax.rem(me + k, n)
            p_z, p_y = p // cores, lax.rem(p, cores)
            far = relayed(p_z, p_y, z, y)

            @pl.when(far)
            def _():
                copy = remote(
                    source(p), relay.at[z], sems.at[0, p], relay_sems.at[0, z],
                    relay_dev(p_z, p_y),
                )
                act(copy)

            @pl.when(jnp.logical_not(far))
            def _():
                copy = remote(
                    source(p), final.at[me], sems.at[0, p], sems.at[1, me],
                    {"tp": p_z, "cores": p_y},
                )
                act(copy)

    def relay_copy(final, relay, sems, relay_sems, k):
        s_z = lax.rem(end + k, size)
        s = s_z * cores + other
        return s_z, remote(
            relay.at[s_z], final.at[s], relay_sems.at[1, s_z], sems.at[1, s], {"tp": end}
        )

    def pass_on(final, relay, sems, relay_sems):
        @pl.when(near_end)
        def _():
            for k in range(1, size):
                s_z, copy = relay_copy(final, relay, sems, relay_sems, k)
                remote(
                    relay.at[s_z], relay.at[s_z], relay_sems.at[1, s_z], relay_sems.at[0, s_z],
                    {"tp": end},
                ).wait_recv()
                copy.start()

    def scattered(final, sems):
        for k in range(1, n):
            s = lax.rem(me + k, n)
            remote(final.at[s], final.at[s], sems.at[0, s], sems.at[1, s], y_dev).wait_recv()

    def relays_done(final, relay, sems, relay_sems):
        @pl.when(near_end)
        def _():
            for k in range(1, size):
                relay_copy(final, relay, sems, relay_sems, k)[1].wait_send()

    def started(copy):
        copy.start()

    def sent(copy):
        copy.wait_send()

    def u_source(p):
        return up.at[p]

    def u_scatter(act):
        scatter(u_source, u1, u_relay, u1_sem, ur_sem, act)

    def d_copy(k):
        mine = d_all.at[pl.ds(g * per, per)]
        return remote(down, mine, d_sem.at[0, k], d_sem.at[1, k], peer(k))

    def u2_copy(k):
        return remote(u_pick.at[k], u_all.at[g], u2_sem.at[0, k], u2_sem.at[1, k], peer(k))

    def pick(source, picked, mine):
        for k in range(groups):
            which = lax.rem(g + k, groups)
            for j in range(seg_count):
                value = source[pool_rows[adapters[which, j]]]
                if k:
                    picked[k, j] = value
                else:
                    mine[g, j] = value


    tile_rows = [pool_rows[adapters[g, seg]] for seg in tile_seg]

    def low_send(c):
        base = c * rows
        for t in range(rows // TILE):
            tile = c * (rows // TILE) + t
            value = low[base + t * TILE : base + (t + 1) * TILE]
            value = jnp.where(tile_rows[tile] == me, value, 0.0).astype(part.dtype)
            count = TILE // piece_rows
            for i in range(count):
                part[c, t * count + i] = value[i * piece_rows : (i + 1) * piece_rows]
        for k in range(1, n):
            s_copy(c, k).start()

    def mate(k):
        p = lax.rem(me + k, n)
        return p, {"tp": p // cores, "cores": lax.rem(p, cores)}

    def s_copy(c, k):
        p, dev = mate(k)
        return remote(
            part.at[c, p], s_in.at[c, k], s_sem.at[0, c, k], s_sem.at[1, c, k], dev
        )

    def g_copy(c, k):
        _, dev = mate(k)
        mine = shrunk.at[c, me]
        return remote(mine, mine, g_sem.at[0, c, k], g_sem.at[1, c, k], dev)

    def low_sum(c):
        total = part[c, me].astype(jnp.float32)
        for k in range(1, n):
            s_copy(c, k).wait_recv()
            total = total + s_in[c, k].astype(jnp.float32)
        shrunk[c, me] = total.astype(shrunk.dtype)

    def low_share(c):
        for k in range(1, n):
            g_copy(c, k).start()

    def low_ready(c):
        for k in range(1, n):
            p = lax.rem(me + n - k, n)
            mine = shrunk.at[c, p]
            remote(mine, mine, g_sem.at[0, c, k], g_sem.at[1, c, k], y_dev).wait_recv()

    def here(src, dst, k):
        return pltpu.make_async_copy(src, dst, o_sem.at[k])

    def stage_copy(c):
        return pltpu.make_async_copy(stage.at[c % 2], out.at[span(c)], o_sem.at[4 + c % 2])

    def epilogue(c):
        base = c * rows
        if c >= 2:
            stage_copy(c - 2).wait()

        def one(j, carry):
            at = pl.ds(pl.multiple_of(j * cols, cols), cols)
            m = (j * cols) // narrow
            offset = lax.rem(j * cols, narrow)
            for t in range(rows // TILE):
                tile = c * (rows // TILE) + t
                count = TILE // piece_rows
                x = shrunk[c, t * count : (t + 1) * count].reshape(TILE, 2 * rank)
                both = []
                for h in range(2):
                    delta = jnp.dot(
                        x[:, h * rank : (h + 1) * rank],
                        u_all[
                            m,
                            tile_seg[tile],
                            :,
                            pl.ds(pl.multiple_of(h * narrow + offset, cols), cols),
                        ],
                        preferred_element_type=jnp.float32,
                    )
                    total = acc[h, base + t * TILE : base + (t + 1) * TILE, at]
                    both.append(total + adapter_scale * delta)
                gate, lift = both
                value = gate / (1.0 + jnp.exp(-gate)) * lift
                stage[c % 2, t * TILE : (t + 1) * TILE, at] = value.astype(stage.dtype)
            return carry

        lax.fori_loop(0, blocks, one, 0)
        stage_copy(c).start()

    def drain(i, carry):
        t, c = i // CHUNKS, lax.rem(i, CHUNKS)
        s, across = t * cores + y, t * cores + other

        def done(s, sems, dev):
            hop(xg.at[s, span(c)], s, c, sems, dev).wait_send()

        @pl.when((z + 1 < size) & (t <= z))
        def _():
            done(s, up_sem, up_dev)

        @pl.when((z >= 1) & (t >= z))
        def _():
            done(s, dn_sem, dn_dev)

        near = (t == z - 1) | (t == z + 1)

        @pl.when(jnp.logical_not(near & shifted(size, t, z, c)))
        def _():
            done(s, y_sem, y_dev)

        @pl.when((t == z) & (z + 1 < size) & shifted(size, z, z + 1, c))
        def _():
            done(across, up_sem, up_dev)

        @pl.when((t == z) & (z >= 1) & shifted(size, z, z - 1, c))
        def _():
            done(across, dn_sem, dn_dev)

        return carry

    def all_sent():
        for k in range(1, groups):
            d_copy(k).wait_send()
            u2_copy(k).wait_send()
        u_scatter(sent)
        relays_done(u1, u_relay, u1_sem, ur_sem)
        lax.fori_loop(0, size * CHUNKS, drain, 0)

    def row_piece(i):
        return table(order, z, i) * cores + y

    def cross_piece(i):
        return table(order, z, i) * cores + other

    def near_arrivals(c):
        row_arrival(1, c, True)
        mate_arrival(c)

    def cross_ready(piece):
        for c in range(CHUNKS):
            arrived(piece, c)

    far = cross_piece(size - 1)


    for c in range(CHUNKS):
        send_row(c)
        send_mate(c)
    for k in range(1, groups):
        d_copy(k).start()
    here(down, d_all.at[pl.ds(g * per, per)], 0).start()
    here(up.at[me], u1.at[me], 1).start()
    u_scatter(started)
    run_round(
        [me], [tokens], True, False,
        [functools.partial(near_arrivals, c) for c in range(CHUNKS)],
    )
    here(down, d_all.at[pl.ds(g * per, per)], 0).wait()
    for k in range(1, groups):
        d_copy(k).wait_recv()
    low[...] = jnp.dot(xv[0], d_all[me], preferred_element_type=jnp.float32)
    pair = [row_piece(1), cross_piece(0)]
    run_round(pair, [xg.at[q] for q in pair])
    pass_on(u1, u_relay, u1_sem, ur_sem)
    row_arrival(2, 0, False)
    cross_ready(cross_piece(1))
    run_round(
        [cross_piece(1)], [xg.at[cross_piece(1)]],
        hooks=[functools.partial(row_arrival, 2, c, False) for c in range(1, CHUNKS - 1)],
    )
    here(up.at[me], u1.at[me], 1).wait()
    scattered(u1, u1_sem)
    pick(u1, u_pick, u_all)
    row_arrival(2, CHUNKS - 1, False)
    for k in range(1, groups):
        u2_copy(k).start()
    run_round(
        [row_piece(2)], [xg.at[row_piece(2)]],
        hooks=[functools.partial(row_arrival, 3, 0, False)],
    )
    cross_ready(cross_piece(2))
    run_round(
        [cross_piece(2)], [xg.at[cross_piece(2)]],
        hooks=[functools.partial(row_arrival, 3, 1, False)],
    )
    for c in range(2, CHUNKS):
        row_arrival(3, c, False)
    run_round([row_piece(3)], [xg.at[row_piece(3)]])


    def low_far(c):
        at = pl.ds(c * rows, rows)
        arrived(far, c)
        copy = pltpu.make_async_copy(xg.at[far, span(c)], xv.at[0, at], x_sem.at[0])
        copy.start()
        copy.wait()
        term = jnp.dot(xv[0, at], d_all[far], preferred_element_type=jnp.float32)
        low[at] = low[at] + term
        low_send(c)

    def far_product(low_row, count):
        def one(j, carry):
            multiply([far], j, low_row, count, False)
            return carry

        lax.fori_loop(0, blocks, one, 0)

    first_tiles([far])
    for c in range(CHUNKS - 1):
        low_far(c)
    far_product(0, token_count - rows)
    for c in range(CHUNKS - 1):
        low_sum(c)
    for k in range(1, groups):
        u2_copy(k).wait_recv()
    for c in range(CHUNKS - 1):
        low_share(c)
    first_tiles([far])
    for c in range(CHUNKS - 2):
        low_ready(c)
        epilogue(c)
    all_sent()
    low_far(CHUNKS - 1)
    far_product(token_count - rows, rows)
    low_sum(CHUNKS - 1)
    low_ready(CHUNKS - 2)
    low_share(CHUNKS - 1)
    epilogue(CHUNKS - 2)
    low_ready(CHUNKS - 1)
    epilogue(CHUNKS - 1)
    for c in range(CHUNKS):
        for k in range(1, n):
            s_copy(c, k).wait_send()
            g_copy(c, k).wait_send()
    for c in range(max(0, CHUNKS - 2), CHUNKS):
        stage_copy(c).wait()


def fused_call(counts, adapters, pool_rows, tokens, weight, down, up, groups, size, cores):
    n = size * cores
    token_count, depth = tokens.shape
    hidden = weight.shape[2]
    cols = min(BLOCK_COLS, hidden)
    twice_rank = down.shape[-1]
    rows = token_count // CHUNKS
    segs = adapters.shape[1]
    dma = pltpu.SemaphoreType.DMA
    any_space = pl.BlockSpec(memory_space=pl.ANY)
    smem = pl.BlockSpec(memory_space=pltpu.SMEM)
    leaf = up.shape[1:]
    vmem = pltpu.VMEM
    return pl.pallas_call(
        fused_kernel,
        out_shape=(
            jax.ShapeDtypeStruct((n, token_count, depth), tokens.dtype),
            jax.ShapeDtypeStruct((token_count, hidden), jnp.bfloat16),
        ),
        in_specs=[smem] * 3 + [any_space] * 4,
        out_specs=(any_space,) * 2,
        scratch_shapes=[
            vmem((2, token_count, hidden), jnp.float32),
            vmem((2, token_count, depth), tokens.dtype),
            vmem((2, 2, depth, 2, cols), weight.dtype),
            vmem((n, depth, twice_rank), down.dtype),
            vmem((token_count, twice_rank), jnp.float32),
            vmem((n,) + leaf, up.dtype),
            vmem((groups, segs) + leaf, up.dtype),
            vmem((groups, segs) + leaf, up.dtype),
            vmem((size,) + leaf, up.dtype),
            vmem((CHUNKS, n, rows // n, twice_rank), jnp.bfloat16),
            vmem((CHUNKS, n, rows // n, twice_rank), jnp.bfloat16),
            vmem((CHUNKS, n, rows // n, twice_rank), jnp.bfloat16),
            vmem((2, rows, hidden), jnp.bfloat16),
            dma((n, CHUNKS)),
            dma((n, CHUNKS)),
            dma((n, CHUNKS)),
            dma((n, CHUNKS)),
            dma((3,)),
            dma((2, 2)),
            dma((2, groups)),
            dma((2, n)),
            dma((2, groups)),
            dma((2, size)),
            dma((2, CHUNKS, n)),
            dma((2, CHUNKS, n)),
            dma((6,)),
        ],
        compiler_params=pltpu.CompilerParams(
            vmem_limit_bytes=VMEM_LIMIT, has_side_effects=True
        ),
        name="fused",
    )(counts, adapters, pool_rows, tokens, weight, down, up)


def compute_fused(
    tokens,
    gate_up_weight,
    down_factor_pool,
    up_factor_pool,
    segment_adapters,
    segment_tile_counts,
    adapter_pool_rows,
):
    groups = lax.axis_size("grp")
    size, cores = lax.axis_size("tp"), lax.axis_size("cores")
    depth = tokens.shape[1]
    down = down_factor_pool.reshape(size * cores // groups, depth, down_factor_pool.shape[2])
    up = up_factor_pool.reshape(up_factor_pool.shape[2:])
    return fused_call(
        segment_tile_counts,
        segment_adapters,
        adapter_pool_rows,
        tokens,
        gate_up_weight,
        down,
        up,
        groups,
        size,
        cores,
    )[1]


def fits(mesh):
    size, cores, groups = mesh.shape["tp"], mesh.shape["cores"], mesh.shape["grp"]
    return cores == 2 and size == 4 and size * cores % groups == 0


def per_device(*args):
    return compute(*args)


def compute(
    tokens,
    gate_up_weight,
    down_factor_pool,
    up_factor_pool,
    segment_adapters,
    segment_tile_counts,
    adapter_pool_rows,
):
    groups = lax.axis_size("grp")
    tp_size, cores_size = lax.axis_size("tp"), lax.axis_size("cores")
    n = tp_size * cores_size
    token_count, depth = tokens.shape
    local_hidden_width = gate_up_weight.shape[2]
    twice_rank = down_factor_pool.shape[2]
    narrow = local_hidden_width // groups
    seg_count = segment_adapters.shape[1]
    half = token_count // 2

    me = ring_position(lax.axis_index("tp"), lax.axis_index("cores"), tp_size)
    order = [ring_device(k, tp_size, cores_size) for k in range(n)]
    forward = [(order[k], order[(k + 1) % n]) for k in range(n)]
    backward = [(order[(k + 1) % n], order[k]) for k in range(n)]

    def owner(shift):
        return ring_device((me + shift + n) % n, tp_size, cores_size).astype(jnp.int32)

    full_steps = (n - 1) // 2
    lefts, rights = [tokens], [tokens]
    for _ in range(1, full_steps + 1):
        lefts.append(lax.ppermute(lefts[-1], TP, forward))
        rights.append(lax.ppermute(rights[-1], TP, backward))
    last_top = lax.ppermute(lefts[-1][:half], TP, forward)
    last_bottom = lax.ppermute(rights[-1][half:], TP, backward)

    piece = depth // groups
    a = down_factor_pool.reshape(n // groups, groups, piece, twice_rank)
    a = lax.all_to_all(a, "grp", split_axis=1, concat_axis=0, tiled=True)
    a = a.reshape(n, piece, twice_rank)
    a = lax.all_to_all(a, TP, split_axis=0, concat_axis=0, tiled=True)
    b = up_factor_pool.reshape(up_factor_pool.shape[2:])
    b = lax.all_to_all(b, TP, split_axis=0, concat_axis=0, tiled=True)
    slots = jnp.take(adapter_pool_rows, segment_adapters, mode="clip")
    a = group_exchange(a, slots)
    b = group_exchange(b, slots)
    block_cols = narrow
    if narrow % 128:
        block_cols = local_hidden_width
        b = b.reshape(groups, seg_count, b.shape[2], 2, narrow)
        b = jnp.transpose(b, (1, 2, 3, 0, 4))
        b = b.reshape(1, seg_count, b.shape[1], 2 * block_cols)

    tile_count = token_count // TILE
    tile_seg = tile_segments(segment_tile_counts[0], tile_count).astype(jnp.int32)
    row_seg = jnp.repeat(tile_seg, TILE)[:, None]
    partial = None
    for j in range(seg_count):
        term = jnp.dot(
            tokens, a[:, j].reshape(depth, twice_rank), preferred_element_type=jnp.float32
        )
        partial = term if partial is None else jnp.where(row_seg == j, term, partial)
    share = token_count // n
    partial = lax.all_to_all(
        partial.reshape(n, share, twice_rank), TP, split_axis=0, concat_axis=0, tiled=True
    )
    own = jnp.sum(partial, axis=0).astype(jnp.bfloat16)
    shrunk = lax.all_to_all(
        jnp.broadcast_to(own[None], (n, share, twice_rank)),
        TP,
        split_axis=0,
        concat_axis=0,
        tiled=True,
    ).reshape(token_count, twice_rank)

    acc = None
    for s in range(1, full_steps + 1):
        xs = [lefts[s], rights[s]]
        rows = [owner(-s), owner(s)]
        if s == 1:
            xs.insert(0, tokens)
            rows.insert(0, owner(0))
        acc = partial_matmul(xs, gate_up_weight, jnp.stack(rows), acc, block_cols)
    return final_matmul(
        last_top, last_bottom, gate_up_weight, jnp.stack([owner(n // 2)]), acc, shrunk, b, tile_seg
    )


def fused(*args):
    return compute_fused(*args)


def solution(mesh):
    direct = fits(mesh)
    return jax.shard_map(
        fused if direct else per_device,
        mesh=mesh,
        in_specs=(
            P("grp", ("tp", "cores")),
            P(None, None, ("tp", "cores")),
            P(("tp", "cores"), "grp", None),
            P(("tp", "cores"), "grp", None, None, None),
            P(),
            P("grp", None),
            P(),
        ),
        out_specs=P("grp", ("tp", "cores")),
        check_vma=False,
    )
```

```python
import functools

import jax
import jax.numpy as jnp
from jax import lax
from jax.experimental import pallas as pl
from jax.experimental.pallas import tpu as pltpu
from jax.sharding import PartitionSpec as P


TILE = 128
VMEM_LIMIT = 60 * 1024 * 1024

adapter_scale = 0.5


TP = ("tp", "cores")


def tile_segments(tile_lengths, tile_count):
    bounds = jnp.cumsum(tile_lengths)
    positions = jnp.arange(tile_count, dtype=jnp.int32)
    return jnp.sum((bounds[None, :] <= positions[:, None]).astype(jnp.int32), axis=1)


def ring_device(position, tp_size, cores_size):
    c = position // tp_size
    t = position % tp_size
    t = t + (c % 2) * (tp_size - 1 - 2 * t)
    return t * cores_size + c


def ring_position(tp_index, cores_index, tp_size):
    t = tp_index + (cores_index % 2) * (tp_size - 1 - 2 * tp_index)
    return cores_index * tp_size + t


def partial_kernel(count, with_acc, rows_ref, *refs):
    xs, ws = refs[:count], refs[count : 2 * count]
    out = refs[-1]
    ws = [jnp.swapaxes(w[...], 0, 1) for w in ws]
    for h in range(2):
        total = refs[2 * count][h] if with_acc else None
        for x, w in zip(xs, ws):
            term = jnp.dot(x[...], w[h], preferred_element_type=jnp.float32)
            total = term if total is None else total + term
        out[h] = total


def partial_matmul(xs, weight, rows, acc, block_cols):
    count = len(xs)
    tokens, depth = xs[0].shape
    hidden = weight.shape[2]
    block_cols = min(block_cols, 256)
    in_specs = [pl.BlockSpec((tokens, depth), lambda j, r: (0, 0))] * count
    for k in range(count):
        in_specs.append(
            pl.BlockSpec((depth, 2, block_cols), lambda j, r, k=k: (r[k], 0, j))
        )
    acc_spec = pl.BlockSpec((2, tokens, block_cols), lambda j, r: (0, 0, j))
    operands = list(xs) + [weight] * count
    aliases = {}
    if acc is not None:
        in_specs.append(acc_spec)
        aliases = {1 + len(operands): 0}
        operands.append(acc)
    return pl.pallas_call(
        functools.partial(partial_kernel, count, acc is not None),
        out_shape=jax.ShapeDtypeStruct((2, tokens, hidden), jnp.float32),
        grid_spec=pltpu.PrefetchScalarGridSpec(
            num_scalar_prefetch=1,
            grid=(hidden // block_cols,),
            in_specs=in_specs,
            out_specs=acc_spec,
        ),
        input_output_aliases=aliases,
        compiler_params=pltpu.CompilerParams(vmem_limit_bytes=VMEM_LIMIT),
        cost_estimate=pl.CostEstimate(
            flops=4 * count * tokens * depth * hidden,
            bytes_accessed=count * 4 * depth * hidden + 16 * tokens * hidden,
            transcendentals=0,
        ),
    )(rows, *operands)


def final_kernel(tiles_per_half, rank, rows_ref, seg_ref, xt, xb, w, acc, shrunk, b, out, total):
    narrow = out.shape[1]
    w = jnp.swapaxes(w[...], 0, 1)
    for p, x in enumerate((xt, xb)):
        for h in range(2):
            span = slice(p * x.shape[0], (p + 1) * x.shape[0])
            total[h, span] = acc[h, span] + jnp.dot(
                x[...], w[h], preferred_element_type=jnp.float32
            )
        for t in range(p * tiles_per_half, (p + 1) * tiles_per_half):
            seg = seg_ref[t]
            span = slice(t * TILE, (t + 1) * TILE)
            both = []
            for h in range(2):
                delta = jnp.dot(
                    shrunk[span, h * rank : (h + 1) * rank],
                    b[0, seg, :, h * narrow : (h + 1) * narrow],
                    preferred_element_type=jnp.float32,
                )
                both.append(total[h, span] + adapter_scale * delta)
            gate, up = both
            out[span] = (gate / (1.0 + jnp.exp(-gate)) * up).astype(out.dtype)


def final_matmul(xt, xb, weight, rows, acc, shrunk, b_chosen, tile_seg):
    half, depth = xt.shape
    tokens = 2 * half
    hidden = weight.shape[2]
    blocks, segs, rank, twice = b_chosen.shape
    narrow = twice // 2
    return pl.pallas_call(
        functools.partial(final_kernel, half // TILE, rank),
        out_shape=jax.ShapeDtypeStruct((tokens, hidden), jnp.bfloat16),
        grid_spec=pltpu.PrefetchScalarGridSpec(
            num_scalar_prefetch=2,
            grid=(blocks,),
            in_specs=[
                pl.BlockSpec((half, depth), lambda j, r, s: (0, 0)),
                pl.BlockSpec((half, depth), lambda j, r, s: (0, 0)),
                pl.BlockSpec((depth, 2, narrow), lambda j, r, s: (r[0], 0, j)),
                pl.BlockSpec((2, tokens, narrow), lambda j, r, s: (0, 0, j)),
                pl.BlockSpec((tokens, 2 * rank), lambda j, r, s: (0, 0)),
                pl.BlockSpec((1, segs, rank, twice), lambda j, r, s: (j, 0, 0, 0)),
            ],
            out_specs=pl.BlockSpec((tokens, narrow), lambda j, r, s: (0, j)),
            scratch_shapes=[pltpu.VMEM((2, tokens, narrow), jnp.float32)],
        ),
        compiler_params=pltpu.CompilerParams(vmem_limit_bytes=VMEM_LIMIT),
        cost_estimate=pl.CostEstimate(
            flops=4 * tokens * (depth + rank) * hidden,
            bytes_accessed=4 * depth * hidden + 10 * tokens * hidden,
            transcendentals=tokens * hidden,
        ),
    )(rows, tile_seg, xt, xb, weight, acc, shrunk, b_chosen)


def group_exchange(pool, slots):
    groups = lax.axis_size("grp")
    g = lax.axis_index("grp")
    parts = []
    for k in range(groups):
        wanted = lax.dynamic_index_in_dim(slots, (g + k) % groups, 0, keepdims=False)
        part = jnp.take(pool, wanted, axis=0, mode="clip")
        if k:
            pairs = [(i, (i + k) % groups) for i in range(groups)]
            part = lax.ppermute(part, "grp", pairs)
        parts.append(part)
    sources = (g + groups - jnp.arange(groups)) % groups
    return jnp.take(jnp.stack(parts), sources, axis=0, mode="clip")


MESH = pl.DeviceIdType.MESH
CHUNKS = 4
END_SHIFT = 0
BLOCK_COLS = 512


def table(rows, i, k):
    total = 0
    for a, row in enumerate(rows):
        for b, value in enumerate(row):
            if value:
                total = total + jnp.where((i == a) & (k == b), value, 0)
    return total


def reach(size):
    return [sorted(range(size), key=lambda t, z=z: (abs(t - z), t)) for z in range(size)]


def shifted(size, source, dest, c):
    to_end = ((dest == 0) | (dest == size - 1)) & (c >= CHUNKS - END_SHIFT)
    from_end = (source == 0) | (source == size - 1)
    return to_end | from_end


def fused_kernel(
    counts,
    adapters,
    pool_rows,
    tokens,
    weight,
    down,
    up,
    xg,
    out,
    acc,
    xv,
    wbuf,
    d_all,
    low,
    u1,
    u_pick,
    u_all,
    u_relay,
    part,
    s_in,
    shrunk,
    stage,
    recv,
    up_sem,
    dn_sem,
    y_sem,
    x_sem,
    w_sem,
    d_sem,
    u1_sem,
    u2_sem,
    ur_sem,
    s_sem,
    g_sem,
    o_sem,
):
    groups = lax.axis_size("grp")
    size, cores = lax.axis_size("tp"), lax.axis_size("cores")
    n = size * cores
    g, z, y = lax.axis_index("grp"), lax.axis_index("tp"), lax.axis_index("cores")
    me = z * cores + y
    other = 1 - y
    token_count, depth = tokens.shape
    rows = token_count // CHUNKS
    hidden = weight.shape[2]
    cols = wbuf.shape[-1]
    blocks = hidden // cols
    per = n // groups
    order = reach(size)
    seg_count = adapters.shape[1]
    rank = up.shape[1]
    narrow = up.shape[2] // 2
    piece_rows = rows // n

    ends = []
    for k in range(seg_count):
        ends.append(counts[0, k] + (ends[-1] if ends else 0))
    tile_seg = []
    for t in range(token_count // TILE):
        seg = 0
        for k in range(seg_count - 1):
            seg = seg + jnp.where(ends[k] <= t, 1, 0)
        tile_seg.append(seg)

    def peer(k):
        return {"grp": lax.rem(g + k, groups)}

    def span(c):
        if isinstance(c, int):
            return pl.ds(c * rows, rows)
        return pl.ds(pl.multiple_of(c * rows, rows), rows)

    def remote(src, dst, send, receive, dev):
        return pltpu.make_async_remote_copy(
            src_ref=src,
            dst_ref=dst,
            send_sem=send,
            recv_sem=receive,
            device_id=dev,
            device_id_type=MESH,
        )


    def hop(src, s, c, sems, dev):
        return remote(src, xg.at[s, span(c)], sems.at[s, c], recv.at[s, c], dev)

    up_dev, dn_dev, y_dev = {"tp": z + 1}, {"tp": z - 1}, {"cores": other}

    def arrived(s, c):
        hop(xg.at[s, span(c)], s, c, y_sem, y_dev).wait_recv()

    def forward(s, c, sems, dev):
        hop(xg.at[s, span(c)], s, c, sems, dev).start()

    def send_row(c):
        src = tokens.at[span(c)]

        @pl.when(z + 1 < size)
        def _():
            hop(src, me, c, up_sem, up_dev).start()

        @pl.when(z >= 1)
        def _():
            hop(src, me, c, dn_sem, dn_dev).start()

    def send_mate(c):
        hop(tokens.at[span(c)], me, c, y_sem, y_dev).start()

    def row_arrival(r, c, first):
        lo, hi = z - r, z + r

        @pl.when(lo >= 0)
        def _():
            s = lo * cores + y
            arrived(s, c)

            @pl.when(z + 1 < size)
            def _():
                forward(s, c, up_sem, up_dev)

            @pl.when(jnp.logical_not(shifted(size, lo, z, c)) if first else z >= 0)
            def _():
                forward(s, c, y_sem, y_dev)

        @pl.when(hi < size)
        def _():
            s = hi * cores + y
            arrived(s, c)

            @pl.when(z >= 1)
            def _():
                forward(s, c, dn_sem, dn_dev)

            @pl.when(jnp.logical_not(shifted(size, hi, z, c)) if first else z >= 0)
            def _():
                forward(s, c, y_sem, y_dev)

    def mate_arrival(c):
        s = z * cores + other
        arrived(s, c)

        @pl.when((z + 1 < size) & shifted(size, z, z + 1, c))
        def _():
            forward(s, c, up_sem, up_dev)

        @pl.when((z >= 1) & shifted(size, z, z - 1, c))
        def _():
            forward(s, c, dn_sem, dn_dev)


    def w_copy(piece, j, slot, k):
        return pltpu.make_async_copy(
            weight.at[
                pl.ds(pl.multiple_of(piece * depth, depth), depth),
                slice(None),
                pl.ds(pl.multiple_of(j * cols, cols), cols),
            ],
            wbuf.at[slot, k],
            w_sem.at[slot, k],
        )

    def first_tiles(pieces):
        for k, piece in enumerate(pieces):
            w_copy(piece, 0, 0, k).start()

    def multiply(pieces, j, low_row, count, first):
        slot = lax.rem(j, 2)

        @pl.when(j + 1 < blocks)
        def _():
            for k, piece in enumerate(pieces):
                w_copy(piece, j + 1, 1 - slot, k).start()

        at = pl.ds(pl.multiple_of(j * cols, cols), cols)
        where = pl.ds(low_row, count)
        for k, piece in enumerate(pieces):
            w_copy(piece, j, slot, k).wait()
        ws = [jnp.swapaxes(wbuf[slot, k], 0, 1) for k in range(len(pieces))]
        for h in range(2):
            total = None if first else acc[h, where, at]
            for k in range(len(pieces)):
                term = jnp.dot(xv[k, where], ws[k][h], preferred_element_type=jnp.float32)
                total = term if total is None else total + term
            acc[h, where, at] = total

    def run_round(pieces, sources, first=False, project=True, hooks=(), start=0, count=None):
        count = token_count if count is None else count
        at = pl.ds(start, count)
        first_tiles(pieces)
        copies = [
            pltpu.make_async_copy(src.at[at], xv.at[k, at], x_sem.at[k])
            for k, src in enumerate(sources)
        ]
        for copy in copies:
            copy.start()
        for copy in copies:
            copy.wait()
        if project:
            for k, piece in enumerate(pieces):
                low[at] = low[at] + jnp.dot(
                    xv[k, at], d_all[piece], preferred_element_type=jnp.float32
                )

        def one(j, carry):
            multiply(pieces, j, start, count, first)
            for i, hook in enumerate(hooks):
                if hook is not None:
                    pl.when(j == (i + 1) * blocks // len(hooks) - 1)(hook)
            return carry

        lax.fori_loop(0, blocks, one, 0)


    near_end = (z == 1) | (z == size - 2)
    end = jnp.where(z == 1, 0, size - 1)

    def relayed(p_z, p_y, s_z, s_y):
        return ((p_z == 0) | (p_z == size - 1)) & (p_y != s_y) & (p_z != s_z)

    def relay_dev(p_z, p_y):
        return {"tp": jnp.where(p_z == 0, 1, size - 2), "cores": p_y}

    def scatter(source, final, relay, sems, relay_sems, act):
        for k in range(1, n):
            p = lax.rem(me + k, n)
            p_z, p_y = p // cores, lax.rem(p, cores)
            far = relayed(p_z, p_y, z, y)

            @pl.when(far)
            def _():
                copy = remote(
                    source(p), relay.at[z], sems.at[0, p], relay_sems.at[0, z],
                    relay_dev(p_z, p_y),
                )
                act(copy)

            @pl.when(jnp.logical_not(far))
            def _():
                copy = remote(
                    source(p), final.at[me], sems.at[0, p], sems.at[1, me],
                    {"tp": p_z, "cores": p_y},
                )
                act(copy)

    def relay_copy(final, relay, sems, relay_sems, k):
        s_z = lax.rem(end + k, size)
        s = s_z * cores + other
        return s_z, remote(
            relay.at[s_z], final.at[s], relay_sems.at[1, s_z], sems.at[1, s], {"tp": end}
        )

    def pass_on(final, relay, sems, relay_sems):
        @pl.when(near_end)
        def _():
            for k in range(1, size):
                s_z, copy = relay_copy(final, relay, sems, relay_sems, k)
                remote(
                    relay.at[s_z], relay.at[s_z], relay_sems.at[1, s_z], relay_sems.at[0, s_z],
                    {"tp": end},
                ).wait_recv()
                copy.start()

    def scattered(final, sems):
        for k in range(1, n):
            s = lax.rem(me + k, n)
            remote(final.at[s], final.at[s], sems.at[0, s], sems.at[1, s], y_dev).wait_recv()

    def relays_done(final, relay, sems, relay_sems):
        @pl.when(near_end)
        def _():
            for k in range(1, size):
                relay_copy(final, relay, sems, relay_sems, k)[1].wait_send()

    def started(copy):
        copy.start()

    def sent(copy):
        copy.wait_send()

    def u_source(p):
        return up.at[p]

    def u_scatter(act):
        scatter(u_source, u1, u_relay, u1_sem, ur_sem, act)

    def d_copy(k):
        mine = d_all.at[pl.ds(g * per, per)]
        return remote(down, mine, d_sem.at[0, k], d_sem.at[1, k], peer(k))

    def u2_copy(k):
        return remote(u_pick.at[k], u_all.at[g], u2_sem.at[0, k], u2_sem.at[1, k], peer(k))

    def pick(source, picked, mine):
        for k in range(groups):
            which = lax.rem(g + k, groups)
            for j in range(seg_count):
                value = source[pool_rows[adapters[which, j]]]
                if k:
                    picked[k, j] = value
                else:
                    mine[g, j] = value


    tile_rows = [pool_rows[adapters[g, seg]] for seg in tile_seg]

    def low_send(c):
        base = c * rows
        for t in range(rows // TILE):
            tile = c * (rows // TILE) + t
            value = low[base + t * TILE : base + (t + 1) * TILE]
            value = jnp.where(tile_rows[tile] == me, value, 0.0).astype(part.dtype)
            count = TILE // piece_rows
            for i in range(count):
                part[c, t * count + i] = value[i * piece_rows : (i + 1) * piece_rows]
        for k in range(1, n):
            s_copy(c, k).start()

    def mate(k):
        p = lax.rem(me + k, n)
        return p, {"tp": p // cores, "cores": lax.rem(p, cores)}

    def s_copy(c, k):
        p, dev = mate(k)
        return remote(
            part.at[c, p], s_in.at[c, k], s_sem.at[0, c, k], s_sem.at[1, c, k], dev
        )

    def g_copy(c, k):
        _, dev = mate(k)
        mine = shrunk.at[c, me]
        return remote(mine, mine, g_sem.at[0, c, k], g_sem.at[1, c, k], dev)

    def low_sum(c):
        total = part[c, me].astype(jnp.float32)
        for k in range(1, n):
            s_copy(c, k).wait_recv()
            total = total + s_in[c, k].astype(jnp.float32)
        shrunk[c, me] = total.astype(shrunk.dtype)

    def low_share(c):
        for k in range(1, n):
            g_copy(c, k).start()

    def low_ready(c):
        for k in range(1, n):
            p = lax.rem(me + n - k, n)
            mine = shrunk.at[c, p]
            remote(mine, mine, g_sem.at[0, c, k], g_sem.at[1, c, k], y_dev).wait_recv()

    def here(src, dst, k):
        return pltpu.make_async_copy(src, dst, o_sem.at[k])

    def stage_copy(c):
        return pltpu.make_async_copy(stage.at[c % 2], out.at[span(c)], o_sem.at[4 + c % 2])

    def epilogue(c):
        base = c * rows
        if c >= 2:
            stage_copy(c - 2).wait()

        def one(j, carry):
            at = pl.ds(pl.multiple_of(j * cols, cols), cols)
            m = (j * cols) // narrow
            offset = lax.rem(j * cols, narrow)
            for t in range(rows // TILE):
                tile = c * (rows // TILE) + t
                count = TILE // piece_rows
                x = shrunk[c, t * count : (t + 1) * count].reshape(TILE, 2 * rank)
                both = []
                for h in range(2):
                    delta = jnp.dot(
                        x[:, h * rank : (h + 1) * rank],
                        u_all[
                            m,
                            tile_seg[tile],
                            :,
                            pl.ds(pl.multiple_of(h * narrow + offset, cols), cols),
                        ],
                        preferred_element_type=jnp.float32,
                    )
                    total = acc[h, base + t * TILE : base + (t + 1) * TILE, at]
                    both.append(total + adapter_scale * delta)
                gate, lift = both
                value = gate / (1.0 + jnp.exp(-gate)) * lift
                stage[c % 2, t * TILE : (t + 1) * TILE, at] = value.astype(stage.dtype)
            return carry

        lax.fori_loop(0, blocks, one, 0)
        stage_copy(c).start()

    def drain(i, carry):
        t, c = i // CHUNKS, lax.rem(i, CHUNKS)
        s, across = t * cores + y, t * cores + other

        def done(s, sems, dev):
            hop(xg.at[s, span(c)], s, c, sems, dev).wait_send()

        @pl.when((z + 1 < size) & (t <= z))
        def _():
            done(s, up_sem, up_dev)

        @pl.when((z >= 1) & (t >= z))
        def _():
            done(s, dn_sem, dn_dev)

        near = (t == z - 1) | (t == z + 1)

        @pl.when(jnp.logical_not(near & shifted(size, t, z, c)))
        def _():
            done(s, y_sem, y_dev)

        @pl.when((t == z) & (z + 1 < size) & shifted(size, z, z + 1, c))
        def _():
            done(across, up_sem, up_dev)

        @pl.when((t == z) & (z >= 1) & shifted(size, z, z - 1, c))
        def _():
            done(across, dn_sem, dn_dev)

        return carry

    def all_sent():
        for k in range(1, groups):
            d_copy(k).wait_send()
            u2_copy(k).wait_send()
        u_scatter(sent)
        relays_done(u1, u_relay, u1_sem, ur_sem)
        lax.fori_loop(0, size * CHUNKS, drain, 0)

    def row_piece(i):
        return table(order, z, i) * cores + y

    def cross_piece(i):
        return table(order, z, i) * cores + other

    def near_arrivals(c):
        row_arrival(1, c, True)
        mate_arrival(c)

    def cross_ready(piece):
        for c in range(CHUNKS):
            arrived(piece, c)

    far = cross_piece(size - 1)


    for c in range(CHUNKS):
        send_row(c)
        send_mate(c)
    for k in range(1, groups):
        d_copy(k).start()
    here(down, d_all.at[pl.ds(g * per, per)], 0).start()
    here(up.at[me], u1.at[me], 1).start()
    u_scatter(started)
    run_round(
        [me], [tokens], True, False,
        [functools.partial(near_arrivals, c) for c in range(CHUNKS)],
    )
    here(down, d_all.at[pl.ds(g * per, per)], 0).wait()
    for k in range(1, groups):
        d_copy(k).wait_recv()
    low[...] = jnp.dot(xv[0], d_all[me], preferred_element_type=jnp.float32)
    pair = [row_piece(1), cross_piece(0)]
    run_round(pair, [xg.at[q] for q in pair])
    pass_on(u1, u_relay, u1_sem, ur_sem)
    row_arrival(2, 0, False)
    cross_ready(cross_piece(1))
    run_round(
        [cross_piece(1)], [xg.at[cross_piece(1)]],
        hooks=[functools.partial(row_arrival, 2, c, False) for c in range(1, CHUNKS - 1)],
    )
    here(up.at[me], u1.at[me], 1).wait()
    scattered(u1, u1_sem)
    pick(u1, u_pick, u_all)
    row_arrival(2, CHUNKS - 1, False)
    for k in range(1, groups):
        u2_copy(k).start()
    run_round(
        [row_piece(2)], [xg.at[row_piece(2)]],
        hooks=[functools.partial(row_arrival, 3, 0, False)],
    )
    cross_ready(cross_piece(2))
    run_round(
        [cross_piece(2)], [xg.at[cross_piece(2)]],
        hooks=[functools.partial(row_arrival, 3, 1, False)],
    )
    top = token_count // 2
    run_round(
        [row_piece(3)], [xg.at[row_piece(3)]], start=0, count=top,
        hooks=[functools.partial(row_arrival, 3, 2, False)],
    )


    def low_far(c):
        at = pl.ds(c * rows, rows)
        arrived(far, c)
        copy = pltpu.make_async_copy(xg.at[far, span(c)], xv.at[0, at], x_sem.at[0])
        copy.start()
        copy.wait()
        term = jnp.dot(xv[0, at], d_all[far], preferred_element_type=jnp.float32)
        low[at] = low[at] + term
        low_send(c)

    def far_product(low_row, count, hook=None):
        def one(j, carry):
            multiply([far], j, low_row, count, False)
            if hook is not None:
                pl.when(j == blocks // 2 - 1)(hook)
            return carry

        lax.fori_loop(0, blocks, one, 0)

    first_tiles([far])
    low_far(0)
    low_far(1)
    far_product(0, top, functools.partial(row_arrival, 3, 3, False))
    run_round([row_piece(3)], [xg.at[row_piece(3)]], start=top, count=top)
    first_tiles([far])
    low_sum(0)
    low_sum(1)
    low_far(2)
    low_share(0)
    low_share(1)
    far_product(top, rows)
    for k in range(1, groups):
        u2_copy(k).wait_recv()
    first_tiles([far])
    low_sum(2)
    low_ready(0)
    epilogue(0)
    low_share(2)
    low_ready(1)
    epilogue(1)
    low_far(3)
    far_product(top + rows, rows)
    low_sum(3)
    low_ready(2)
    low_share(3)
    epilogue(2)
    all_sent()
    low_ready(3)
    epilogue(3)
    for c in range(CHUNKS):
        for k in range(1, n):
            s_copy(c, k).wait_send()
            g_copy(c, k).wait_send()
    for c in range(CHUNKS - 2, CHUNKS):
        stage_copy(c).wait()


def fused_call(counts, adapters, pool_rows, tokens, weight, down, up, groups, size, cores):
    n = size * cores
    token_count, depth = tokens.shape
    hidden = weight.shape[2]
    cols = min(BLOCK_COLS, hidden)
    twice_rank = down.shape[-1]
    rows = token_count // CHUNKS
    segs = adapters.shape[1]
    dma = pltpu.SemaphoreType.DMA
    any_space = pl.BlockSpec(memory_space=pl.ANY)
    smem = pl.BlockSpec(memory_space=pltpu.SMEM)
    leaf = up.shape[1:]
    vmem = pltpu.VMEM
    return pl.pallas_call(
        fused_kernel,
        out_shape=(
            jax.ShapeDtypeStruct((n, token_count, depth), tokens.dtype),
            jax.ShapeDtypeStruct((token_count, hidden), jnp.bfloat16),
        ),
        in_specs=[smem] * 3 + [any_space] * 4,
        out_specs=(any_space,) * 2,
        scratch_shapes=[
            vmem((2, token_count, hidden), jnp.float32),
            vmem((2, token_count, depth), tokens.dtype),
            vmem((2, 2, depth, 2, cols), weight.dtype),
            vmem((n, depth, twice_rank), down.dtype),
            vmem((token_count, twice_rank), jnp.float32),
            vmem((n,) + leaf, up.dtype),
            vmem((groups, segs) + leaf, up.dtype),
            vmem((groups, segs) + leaf, up.dtype),
            vmem((size,) + leaf, up.dtype),
            vmem((CHUNKS, n, rows // n, twice_rank), jnp.bfloat16),
            vmem((CHUNKS, n, rows // n, twice_rank), jnp.bfloat16),
            vmem((CHUNKS, n, rows // n, twice_rank), jnp.bfloat16),
            vmem((2, rows, hidden), jnp.bfloat16),
            dma((n, CHUNKS)),
            dma((n, CHUNKS)),
            dma((n, CHUNKS)),
            dma((n, CHUNKS)),
            dma((3,)),
            dma((2, 2)),
            dma((2, groups)),
            dma((2, n)),
            dma((2, groups)),
            dma((2, size)),
            dma((2, CHUNKS, n)),
            dma((2, CHUNKS, n)),
            dma((6,)),
        ],
        compiler_params=pltpu.CompilerParams(
            vmem_limit_bytes=VMEM_LIMIT, has_side_effects=True
        ),
        name="fused",
    )(counts, adapters, pool_rows, tokens, weight, down, up)


def compute_fused(
    tokens,
    gate_up_weight,
    down_factor_pool,
    up_factor_pool,
    segment_adapters,
    segment_tile_counts,
    adapter_pool_rows,
):
    groups = lax.axis_size("grp")
    size, cores = lax.axis_size("tp"), lax.axis_size("cores")
    depth = tokens.shape[1]
    down = down_factor_pool.reshape(size * cores // groups, depth, down_factor_pool.shape[2])
    up = up_factor_pool.reshape(up_factor_pool.shape[2:])
    return fused_call(
        segment_tile_counts,
        segment_adapters,
        adapter_pool_rows,
        tokens,
        gate_up_weight,
        down,
        up,
        groups,
        size,
        cores,
    )[1]


def fits(mesh):
    size, cores, groups = mesh.shape["tp"], mesh.shape["cores"], mesh.shape["grp"]
    return cores == 2 and size == 4 and size * cores % groups == 0


def per_device(*args):
    return compute(*args)


def compute(
    tokens,
    gate_up_weight,
    down_factor_pool,
    up_factor_pool,
    segment_adapters,
    segment_tile_counts,
    adapter_pool_rows,
):
    groups = lax.axis_size("grp")
    tp_size, cores_size = lax.axis_size("tp"), lax.axis_size("cores")
    n = tp_size * cores_size
    token_count, depth = tokens.shape
    local_hidden_width = gate_up_weight.shape[2]
    twice_rank = down_factor_pool.shape[2]
    narrow = local_hidden_width // groups
    seg_count = segment_adapters.shape[1]
    half = token_count // 2

    me = ring_position(lax.axis_index("tp"), lax.axis_index("cores"), tp_size)
    order = [ring_device(k, tp_size, cores_size) for k in range(n)]
    forward = [(order[k], order[(k + 1) % n]) for k in range(n)]
    backward = [(order[(k + 1) % n], order[k]) for k in range(n)]

    def owner(shift):
        return ring_device((me + shift + n) % n, tp_size, cores_size).astype(jnp.int32)

    full_steps = (n - 1) // 2
    lefts, rights = [tokens], [tokens]
    for _ in range(1, full_steps + 1):
        lefts.append(lax.ppermute(lefts[-1], TP, forward))
        rights.append(lax.ppermute(rights[-1], TP, backward))
    last_top = lax.ppermute(lefts[-1][:half], TP, forward)
    last_bottom = lax.ppermute(rights[-1][half:], TP, backward)

    piece = depth // groups
    a = down_factor_pool.reshape(n // groups, groups, piece, twice_rank)
    a = lax.all_to_all(a, "grp", split_axis=1, concat_axis=0, tiled=True)
    a = a.reshape(n, piece, twice_rank)
    a = lax.all_to_all(a, TP, split_axis=0, concat_axis=0, tiled=True)
    b = up_factor_pool.reshape(up_factor_pool.shape[2:])
    b = lax.all_to_all(b, TP, split_axis=0, concat_axis=0, tiled=True)
    slots = jnp.take(adapter_pool_rows, segment_adapters, mode="clip")
    a = group_exchange(a, slots)
    b = group_exchange(b, slots)
    block_cols = narrow
    if narrow % 128:
        block_cols = local_hidden_width
        b = b.reshape(groups, seg_count, b.shape[2], 2, narrow)
        b = jnp.transpose(b, (1, 2, 3, 0, 4))
        b = b.reshape(1, seg_count, b.shape[1], 2 * block_cols)

    tile_count = token_count // TILE
    tile_seg = tile_segments(segment_tile_counts[0], tile_count).astype(jnp.int32)
    row_seg = jnp.repeat(tile_seg, TILE)[:, None]
    partial = None
    for j in range(seg_count):
        term = jnp.dot(
            tokens, a[:, j].reshape(depth, twice_rank), preferred_element_type=jnp.float32
        )
        partial = term if partial is None else jnp.where(row_seg == j, term, partial)
    share = token_count // n
    partial = lax.all_to_all(
        partial.reshape(n, share, twice_rank), TP, split_axis=0, concat_axis=0, tiled=True
    )
    own = jnp.sum(partial, axis=0).astype(jnp.bfloat16)
    shrunk = lax.all_to_all(
        jnp.broadcast_to(own[None], (n, share, twice_rank)),
        TP,
        split_axis=0,
        concat_axis=0,
        tiled=True,
    ).reshape(token_count, twice_rank)

    acc = None
    for s in range(1, full_steps + 1):
        xs = [lefts[s], rights[s]]
        rows = [owner(-s), owner(s)]
        if s == 1:
            xs.insert(0, tokens)
            rows.insert(0, owner(0))
        acc = partial_matmul(xs, gate_up_weight, jnp.stack(rows), acc, block_cols)
    return final_matmul(
        last_top, last_bottom, gate_up_weight, jnp.stack([owner(n // 2)]), acc, shrunk, b, tile_seg
    )


def fused(*args):
    return compute_fused(*args)


def solution(mesh):
    direct = fits(mesh)
    return jax.shard_map(
        fused if direct else per_device,
        mesh=mesh,
        in_specs=(
            P("grp", ("tp", "cores")),
            P(None, None, ("tp", "cores")),
            P(("tp", "cores"), "grp", None),
            P(("tp", "cores"), "grp", None, None, None),
            P(),
            P("grp", None),
            P(),
        ),
        out_specs=P("grp", ("tp", "cores")),
        check_vma=False,
    )
```

```python
import functools

import jax
import jax.numpy as jnp
from jax import lax
from jax.experimental import pallas as pl
from jax.experimental.pallas import tpu as pltpu
from jax.sharding import PartitionSpec as P


TILE = 128
VMEM_LIMIT = 60 * 1024 * 1024

adapter_scale = 0.5


TP = ("tp", "cores")


def tile_segments(tile_lengths, tile_count):
    bounds = jnp.cumsum(tile_lengths)
    positions = jnp.arange(tile_count, dtype=jnp.int32)
    return jnp.sum((bounds[None, :] <= positions[:, None]).astype(jnp.int32), axis=1)


def ring_device(position, tp_size, cores_size):
    c = position // tp_size
    t = position % tp_size
    t = t + (c % 2) * (tp_size - 1 - 2 * t)
    return t * cores_size + c


def ring_position(tp_index, cores_index, tp_size):
    t = tp_index + (cores_index % 2) * (tp_size - 1 - 2 * tp_index)
    return cores_index * tp_size + t


def partial_kernel(count, with_acc, rows_ref, *refs):
    xs, ws = refs[:count], refs[count : 2 * count]
    out = refs[-1]
    ws = [jnp.swapaxes(w[...], 0, 1) for w in ws]
    for h in range(2):
        total = refs[2 * count][h] if with_acc else None
        for x, w in zip(xs, ws):
            term = jnp.dot(x[...], w[h], preferred_element_type=jnp.float32)
            total = term if total is None else total + term
        out[h] = total


def partial_matmul(xs, weight, rows, acc, block_cols):
    count = len(xs)
    tokens, depth = xs[0].shape
    hidden = weight.shape[2]
    block_cols = min(block_cols, 256)
    in_specs = [pl.BlockSpec((tokens, depth), lambda j, r: (0, 0))] * count
    for k in range(count):
        in_specs.append(
            pl.BlockSpec((depth, 2, block_cols), lambda j, r, k=k: (r[k], 0, j))
        )
    acc_spec = pl.BlockSpec((2, tokens, block_cols), lambda j, r: (0, 0, j))
    operands = list(xs) + [weight] * count
    aliases = {}
    if acc is not None:
        in_specs.append(acc_spec)
        aliases = {1 + len(operands): 0}
        operands.append(acc)
    return pl.pallas_call(
        functools.partial(partial_kernel, count, acc is not None),
        out_shape=jax.ShapeDtypeStruct((2, tokens, hidden), jnp.float32),
        grid_spec=pltpu.PrefetchScalarGridSpec(
            num_scalar_prefetch=1,
            grid=(hidden // block_cols,),
            in_specs=in_specs,
            out_specs=acc_spec,
        ),
        input_output_aliases=aliases,
        compiler_params=pltpu.CompilerParams(vmem_limit_bytes=VMEM_LIMIT),
        cost_estimate=pl.CostEstimate(
            flops=4 * count * tokens * depth * hidden,
            bytes_accessed=count * 4 * depth * hidden + 16 * tokens * hidden,
            transcendentals=0,
        ),
    )(rows, *operands)


def final_kernel(tiles_per_half, rank, rows_ref, seg_ref, xt, xb, w, acc, shrunk, b, out, total):
    narrow = out.shape[1]
    w = jnp.swapaxes(w[...], 0, 1)
    for p, x in enumerate((xt, xb)):
        for h in range(2):
            span = slice(p * x.shape[0], (p + 1) * x.shape[0])
            total[h, span] = acc[h, span] + jnp.dot(
                x[...], w[h], preferred_element_type=jnp.float32
            )
        for t in range(p * tiles_per_half, (p + 1) * tiles_per_half):
            seg = seg_ref[t]
            span = slice(t * TILE, (t + 1) * TILE)
            both = []
            for h in range(2):
                delta = jnp.dot(
                    shrunk[span, h * rank : (h + 1) * rank],
                    b[0, seg, :, h * narrow : (h + 1) * narrow],
                    preferred_element_type=jnp.float32,
                )
                both.append(total[h, span] + adapter_scale * delta)
            gate, up = both
            out[span] = (gate / (1.0 + jnp.exp(-gate)) * up).astype(out.dtype)


def final_matmul(xt, xb, weight, rows, acc, shrunk, b_chosen, tile_seg):
    half, depth = xt.shape
    tokens = 2 * half
    hidden = weight.shape[2]
    blocks, segs, rank, twice = b_chosen.shape
    narrow = twice // 2
    return pl.pallas_call(
        functools.partial(final_kernel, half // TILE, rank),
        out_shape=jax.ShapeDtypeStruct((tokens, hidden), jnp.bfloat16),
        grid_spec=pltpu.PrefetchScalarGridSpec(
            num_scalar_prefetch=2,
            grid=(blocks,),
            in_specs=[
                pl.BlockSpec((half, depth), lambda j, r, s: (0, 0)),
                pl.BlockSpec((half, depth), lambda j, r, s: (0, 0)),
                pl.BlockSpec((depth, 2, narrow), lambda j, r, s: (r[0], 0, j)),
                pl.BlockSpec((2, tokens, narrow), lambda j, r, s: (0, 0, j)),
                pl.BlockSpec((tokens, 2 * rank), lambda j, r, s: (0, 0)),
                pl.BlockSpec((1, segs, rank, twice), lambda j, r, s: (j, 0, 0, 0)),
            ],
            out_specs=pl.BlockSpec((tokens, narrow), lambda j, r, s: (0, j)),
            scratch_shapes=[pltpu.VMEM((2, tokens, narrow), jnp.float32)],
        ),
        compiler_params=pltpu.CompilerParams(vmem_limit_bytes=VMEM_LIMIT),
        cost_estimate=pl.CostEstimate(
            flops=4 * tokens * (depth + rank) * hidden,
            bytes_accessed=4 * depth * hidden + 10 * tokens * hidden,
            transcendentals=tokens * hidden,
        ),
    )(rows, tile_seg, xt, xb, weight, acc, shrunk, b_chosen)


def group_exchange(pool, slots):
    groups = lax.axis_size("grp")
    g = lax.axis_index("grp")
    parts = []
    for k in range(groups):
        wanted = lax.dynamic_index_in_dim(slots, (g + k) % groups, 0, keepdims=False)
        part = jnp.take(pool, wanted, axis=0, mode="clip")
        if k:
            pairs = [(i, (i + k) % groups) for i in range(groups)]
            part = lax.ppermute(part, "grp", pairs)
        parts.append(part)
    sources = (g + groups - jnp.arange(groups)) % groups
    return jnp.take(jnp.stack(parts), sources, axis=0, mode="clip")


MESH = pl.DeviceIdType.MESH
CHUNKS = 4
END_SHIFT = 0
BLOCK_COLS = 512


def table(rows, i, k):
    total = 0
    for a, row in enumerate(rows):
        for b, value in enumerate(row):
            if value:
                total = total + jnp.where((i == a) & (k == b), value, 0)
    return total


def reach(size):
    return [sorted(range(size), key=lambda t, z=z: (abs(t - z), t)) for z in range(size)]


def shifted(size, source, dest, c):
    to_end = ((dest == 0) | (dest == size - 1)) & (c >= CHUNKS - END_SHIFT)
    from_end = (source == 0) | (source == size - 1)
    return to_end | from_end


def fused_kernel(
    counts,
    adapters,
    pool_rows,
    tokens,
    weight,
    down,
    up,
    xg,
    out,
    acc,
    xv,
    wbuf,
    d_all,
    low,
    u1,
    u_pick,
    u_all,
    u_relay,
    part,
    s_in,
    shrunk,
    stage,
    recv,
    up_sem,
    dn_sem,
    y_sem,
    x_sem,
    w_sem,
    d_sem,
    u1_sem,
    u2_sem,
    ur_sem,
    s_sem,
    g_sem,
    o_sem,
):
    groups = lax.axis_size("grp")
    size, cores = lax.axis_size("tp"), lax.axis_size("cores")
    n = size * cores
    g, z, y = lax.axis_index("grp"), lax.axis_index("tp"), lax.axis_index("cores")
    me = z * cores + y
    other = 1 - y
    token_count, depth = tokens.shape
    rows = token_count // CHUNKS
    hidden = weight.shape[2]
    cols = wbuf.shape[-1]
    blocks = hidden // cols
    per = n // groups
    order = reach(size)
    seg_count = adapters.shape[1]
    rank = up.shape[1]
    narrow = up.shape[2] // 2
    piece_rows = rows // n

    ends = []
    for k in range(seg_count):
        ends.append(counts[0, k] + (ends[-1] if ends else 0))
    tile_seg = []
    for t in range(token_count // TILE):
        seg = 0
        for k in range(seg_count - 1):
            seg = seg + jnp.where(ends[k] <= t, 1, 0)
        tile_seg.append(seg)

    def peer(k):
        return {"grp": lax.rem(g + k, groups)}

    def span(c):
        if isinstance(c, int):
            return pl.ds(c * rows, rows)
        return pl.ds(pl.multiple_of(c * rows, rows), rows)

    def remote(src, dst, send, receive, dev):
        return pltpu.make_async_remote_copy(
            src_ref=src,
            dst_ref=dst,
            send_sem=send,
            recv_sem=receive,
            device_id=dev,
            device_id_type=MESH,
        )


    def hop(src, s, c, sems, dev):
        return remote(src, xg.at[s, span(c)], sems.at[s, c], recv.at[s, c], dev)

    up_dev, dn_dev, y_dev = {"tp": z + 1}, {"tp": z - 1}, {"cores": other}

    def arrived(s, c):
        hop(xg.at[s, span(c)], s, c, y_sem, y_dev).wait_recv()

    def forward(s, c, sems, dev):
        hop(xg.at[s, span(c)], s, c, sems, dev).start()

    def send_row(c):
        src = tokens.at[span(c)]

        @pl.when(z + 1 < size)
        def _():
            hop(src, me, c, up_sem, up_dev).start()

        @pl.when(z >= 1)
        def _():
            hop(src, me, c, dn_sem, dn_dev).start()

    def send_mate(c):
        hop(tokens.at[span(c)], me, c, y_sem, y_dev).start()

    def row_arrival(r, c, first):
        lo, hi = z - r, z + r

        @pl.when(lo >= 0)
        def _():
            s = lo * cores + y
            arrived(s, c)

            @pl.when(z + 1 < size)
            def _():
                forward(s, c, up_sem, up_dev)

            @pl.when(jnp.logical_not(shifted(size, lo, z, c)) if first else z >= 0)
            def _():
                forward(s, c, y_sem, y_dev)

        @pl.when(hi < size)
        def _():
            s = hi * cores + y
            arrived(s, c)

            @pl.when(z >= 1)
            def _():
                forward(s, c, dn_sem, dn_dev)

            @pl.when(jnp.logical_not(shifted(size, hi, z, c)) if first else z >= 0)
            def _():
                forward(s, c, y_sem, y_dev)

    def mate_arrival(c):
        s = z * cores + other
        arrived(s, c)

        @pl.when((z + 1 < size) & shifted(size, z, z + 1, c))
        def _():
            forward(s, c, up_sem, up_dev)

        @pl.when((z >= 1) & shifted(size, z, z - 1, c))
        def _():
            forward(s, c, dn_sem, dn_dev)


    def w_copy(piece, j, slot, k):
        return pltpu.make_async_copy(
            weight.at[
                pl.ds(pl.multiple_of(piece * depth, depth), depth),
                slice(None),
                pl.ds(pl.multiple_of(j * cols, cols), cols),
            ],
            wbuf.at[slot, k],
            w_sem.at[slot, k],
        )

    def first_tiles(pieces):
        for k, piece in enumerate(pieces):
            w_copy(piece, 0, 0, k).start()

    def multiply(pieces, j, low_row, count, first, then):
        slot = lax.rem(j, 2)

        @pl.when(j + 1 == blocks)
        def _():
            first_tiles(then)

        @pl.when(j + 1 < blocks)
        def _():
            for k, piece in enumerate(pieces):
                w_copy(piece, j + 1, 1 - slot, k).start()

        at = pl.ds(pl.multiple_of(j * cols, cols), cols)
        where = pl.ds(low_row, count)
        for k, piece in enumerate(pieces):
            w_copy(piece, j, slot, k).wait()
        ws = [jnp.swapaxes(wbuf[slot, k], 0, 1) for k in range(len(pieces))]
        for h in range(2):
            total = None if first else acc[h, where, at]
            for k in range(len(pieces)):
                term = jnp.dot(xv[k, where], ws[k][h], preferred_element_type=jnp.float32)
                total = term if total is None else total + term
            acc[h, where, at] = total

    def run_round(pieces, sources, then, first=False, project=True, hooks=(), start=0, count=None):
        count = token_count if count is None else count
        at = pl.ds(start, count)
        copies = [
            pltpu.make_async_copy(src.at[at], xv.at[k, at], x_sem.at[k])
            for k, src in enumerate(sources)
        ]
        for copy in copies:
            copy.start()
        for copy in copies:
            copy.wait()
        if project:
            for k, piece in enumerate(pieces):
                low[at] = low[at] + jnp.dot(
                    xv[k, at], d_all[piece], preferred_element_type=jnp.float32
                )
        products(pieces, then, first, hooks, start, count)

    def products(pieces, then, first, hooks, start, count):
        def one(j, carry):
            multiply(pieces, j, start, count, first, then)
            for i, hook in enumerate(hooks):
                if hook is not None:
                    pl.when(j == (i + 1) * blocks // len(hooks) - 1)(hook)
            return carry

        lax.fori_loop(0, blocks, one, 0)


    near_end = (z == 1) | (z == size - 2)
    end = jnp.where(z == 1, 0, size - 1)

    def relayed(p_z, p_y, s_z, s_y):
        return ((p_z == 0) | (p_z == size - 1)) & (p_y != s_y) & (p_z != s_z)

    def relay_dev(p_z, p_y):
        return {"tp": jnp.where(p_z == 0, 1, size - 2), "cores": p_y}

    def scatter(source, final, relay, sems, relay_sems, act):
        for k in range(1, n):
            p = lax.rem(me + k, n)
            p_z, p_y = p // cores, lax.rem(p, cores)
            far = relayed(p_z, p_y, z, y)

            @pl.when(far)
            def _():
                copy = remote(
                    source(p), relay.at[z], sems.at[0, p], relay_sems.at[0, z],
                    relay_dev(p_z, p_y),
                )
                act(copy)

            @pl.when(jnp.logical_not(far))
            def _():
                copy = remote(
                    source(p), final.at[me], sems.at[0, p], sems.at[1, me],
                    {"tp": p_z, "cores": p_y},
                )
                act(copy)

    def relay_copy(final, relay, sems, relay_sems, k):
        s_z = lax.rem(end + k, size)
        s = s_z * cores + other
        return s_z, remote(
            relay.at[s_z], final.at[s], relay_sems.at[1, s_z], sems.at[1, s], {"tp": end}
        )

    def pass_on(final, relay, sems, relay_sems):
        @pl.when(near_end)
        def _():
            for k in range(1, size):
                s_z, copy = relay_copy(final, relay, sems, relay_sems, k)
                remote(
                    relay.at[s_z], relay.at[s_z], relay_sems.at[1, s_z], relay_sems.at[0, s_z],
                    {"tp": end},
                ).wait_recv()
                copy.start()

    def scattered(final, sems):
        for k in range(1, n):
            s = lax.rem(me + k, n)
            remote(final.at[s], final.at[s], sems.at[0, s], sems.at[1, s], y_dev).wait_recv()

    def relays_done(final, relay, sems, relay_sems):
        @pl.when(near_end)
        def _():
            for k in range(1, size):
                relay_copy(final, relay, sems, relay_sems, k)[1].wait_send()

    def started(copy):
        copy.start()

    def sent(copy):
        copy.wait_send()

    def u_source(p):
        return up.at[p]

    def u_scatter(act):
        scatter(u_source, u1, u_relay, u1_sem, ur_sem, act)

    def d_copy(k):
        mine = d_all.at[pl.ds(g * per, per)]
        return remote(down, mine, d_sem.at[0, k], d_sem.at[1, k], peer(k))

    def u2_copy(k):
        return remote(u_pick.at[k], u_all.at[g], u2_sem.at[0, k], u2_sem.at[1, k], peer(k))

    def pick(source, picked, mine):
        for k in range(groups):
            which = lax.rem(g + k, groups)
            for j in range(seg_count):
                value = source[pool_rows[adapters[which, j]]]
                if k:
                    picked[k, j] = value
                else:
                    mine[g, j] = value


    tile_rows = [pool_rows[adapters[g, seg]] for seg in tile_seg]

    def low_send(c):
        base = c * rows
        for t in range(rows // TILE):
            tile = c * (rows // TILE) + t
            value = low[base + t * TILE : base + (t + 1) * TILE]
            value = jnp.where(tile_rows[tile] == me, value, 0.0).astype(part.dtype)
            count = TILE // piece_rows
            for i in range(count):
                part[c, t * count + i] = value[i * piece_rows : (i + 1) * piece_rows]
        for k in range(1, n):
            s_copy(c, k).start()

    def mate(k):
        p = lax.rem(me + k, n)
        return p, {"tp": p // cores, "cores": lax.rem(p, cores)}

    def s_copy(c, k):
        p, dev = mate(k)
        return remote(
            part.at[c, p], s_in.at[c, k], s_sem.at[0, c, k], s_sem.at[1, c, k], dev
        )

    def g_copy(c, k):
        _, dev = mate(k)
        mine = shrunk.at[c, me]
        return remote(mine, mine, g_sem.at[0, c, k], g_sem.at[1, c, k], dev)

    def low_sum(c):
        total = part[c, me].astype(jnp.float32)
        for k in range(1, n):
            s_copy(c, k).wait_recv()
            total = total + s_in[c, k].astype(jnp.float32)
        shrunk[c, me] = total.astype(shrunk.dtype)

    def low_share(c):
        for k in range(1, n):
            g_copy(c, k).start()

    def low_ready(c):
        for k in range(1, n):
            p = lax.rem(me + n - k, n)
            mine = shrunk.at[c, p]
            remote(mine, mine, g_sem.at[0, c, k], g_sem.at[1, c, k], y_dev).wait_recv()

    def here(src, dst, k):
        return pltpu.make_async_copy(src, dst, o_sem.at[k])

    def stage_copy(c):
        return pltpu.make_async_copy(stage.at[c % 2], out.at[span(c)], o_sem.at[4 + c % 2])

    def epilogue(c):
        base = c * rows
        if c >= 2:
            stage_copy(c - 2).wait()

        def one(j, carry):
            at = pl.ds(pl.multiple_of(j * cols, cols), cols)
            m = (j * cols) // narrow
            offset = lax.rem(j * cols, narrow)
            for t in range(rows // TILE):
                tile = c * (rows // TILE) + t
                count = TILE // piece_rows
                x = shrunk[c, t * count : (t + 1) * count].reshape(TILE, 2 * rank)
                both = []
                for h in range(2):
                    delta = jnp.dot(
                        x[:, h * rank : (h + 1) * rank],
                        u_all[
                            m,
                            tile_seg[tile],
                            :,
                            pl.ds(pl.multiple_of(h * narrow + offset, cols), cols),
                        ],
                        preferred_element_type=jnp.float32,
                    )
                    total = acc[h, base + t * TILE : base + (t + 1) * TILE, at]
                    both.append(total + adapter_scale * delta)
                gate, lift = both
                value = gate / (1.0 + jnp.exp(-gate)) * lift
                stage[c % 2, t * TILE : (t + 1) * TILE, at] = value.astype(stage.dtype)
            return carry

        lax.fori_loop(0, blocks, one, 0)
        stage_copy(c).start()

    def drain(i, carry):
        t, c = i // CHUNKS, lax.rem(i, CHUNKS)
        s, across = t * cores + y, t * cores + other

        def done(s, sems, dev):
            hop(xg.at[s, span(c)], s, c, sems, dev).wait_send()

        @pl.when((z + 1 < size) & (t <= z))
        def _():
            done(s, up_sem, up_dev)

        @pl.when((z >= 1) & (t >= z))
        def _():
            done(s, dn_sem, dn_dev)

        near = (t == z - 1) | (t == z + 1)

        @pl.when(jnp.logical_not(near & shifted(size, t, z, c)))
        def _():
            done(s, y_sem, y_dev)

        @pl.when((t == z) & (z + 1 < size) & shifted(size, z, z + 1, c))
        def _():
            done(across, up_sem, up_dev)

        @pl.when((t == z) & (z >= 1) & shifted(size, z, z - 1, c))
        def _():
            done(across, dn_sem, dn_dev)

        return carry

    def all_sent():
        for k in range(1, groups):
            d_copy(k).wait_send()
            u2_copy(k).wait_send()
        u_scatter(sent)
        relays_done(u1, u_relay, u1_sem, ur_sem)
        lax.fori_loop(0, size * CHUNKS, drain, 0)

    def row_piece(i):
        return table(order, z, i) * cores + y

    def cross_piece(i):
        return table(order, z, i) * cores + other

    def near_arrivals(c):
        row_arrival(1, c, True)
        mate_arrival(c)

    def cross_ready(piece):
        for c in range(CHUNKS):
            arrived(piece, c)

    far = cross_piece(size - 1)


    for c in range(CHUNKS):
        send_row(c)
        send_mate(c)
    for k in range(1, groups):
        d_copy(k).start()
    here(down, d_all.at[pl.ds(g * per, per)], 0).start()
    here(up.at[me], u1.at[me], 1).start()
    u_scatter(started)
    first_tiles([me])
    pair = [row_piece(1), cross_piece(0)]
    run_round(
        [me], [tokens], pair, True, False,
        [functools.partial(near_arrivals, c) for c in range(CHUNKS)],
    )
    here(down, d_all.at[pl.ds(g * per, per)], 0).wait()
    for k in range(1, groups):
        d_copy(k).wait_recv()
    low[...] = jnp.dot(xv[0], d_all[me], preferred_element_type=jnp.float32)
    run_round(pair, [xg.at[q] for q in pair], [cross_piece(1)])
    pass_on(u1, u_relay, u1_sem, ur_sem)
    row_arrival(2, 0, False)
    cross_ready(cross_piece(1))
    run_round(
        [cross_piece(1)], [xg.at[cross_piece(1)]], [row_piece(2)],
        hooks=[functools.partial(row_arrival, 2, c, False) for c in range(1, CHUNKS - 1)],
    )
    here(up.at[me], u1.at[me], 1).wait()
    scattered(u1, u1_sem)
    pick(u1, u_pick, u_all)
    row_arrival(2, CHUNKS - 1, False)
    for k in range(1, groups):
        u2_copy(k).start()
    near = row_piece(size - 1)
    run_round(
        [row_piece(2)], [xg.at[row_piece(2)]], [cross_piece(2)],
        hooks=[functools.partial(row_arrival, 3, 0, False)],
    )
    cross_ready(cross_piece(2))
    run_round(
        [cross_piece(2)], [xg.at[cross_piece(2)]], [near],
        hooks=[None, None, functools.partial(row_arrival, 3, 1, False), None],
    )
    top = token_count // 2
    run_round(
        [near], [xg.at[near]], [far], start=0, count=top,
        hooks=[functools.partial(row_arrival, 3, 2, False)],
    )


    def low_far(c):
        at = pl.ds(c * rows, rows)
        arrived(far, c)
        copy = pltpu.make_async_copy(xg.at[far, span(c)], xv.at[0, at], x_sem.at[0])
        copy.start()
        copy.wait()
        term = jnp.dot(xv[0, at], d_all[far], preferred_element_type=jnp.float32)
        low[at] = low[at] + term
        low_send(c)

    low_far(0)
    low_far(1)
    products(
        [far], [near], False, [functools.partial(row_arrival, 3, 3, False), None], 0, top
    )
    run_round([near], [xg.at[near]], [far], start=top, count=top)
    low_far(2)
    low_sum(0)
    low_sum(1)
    for k in range(1, groups):
        u2_copy(k).wait_recv()
    low_share(0)
    low_share(1)
    low_far(3)
    products([far], [], False, (), top, top)
    for c in range(2, CHUNKS):
        low_sum(c)
    low_ready(0)
    low_share(2)
    low_share(3)
    epilogue(0)
    low_ready(1)
    epilogue(1)
    all_sent()
    low_ready(2)
    epilogue(2)
    low_ready(3)
    epilogue(3)
    for c in range(CHUNKS):
        for k in range(1, n):
            s_copy(c, k).wait_send()
            g_copy(c, k).wait_send()
    for c in range(CHUNKS - 2, CHUNKS):
        stage_copy(c).wait()


def fused_call(counts, adapters, pool_rows, tokens, weight, down, up, groups, size, cores):
    n = size * cores
    token_count, depth = tokens.shape
    hidden = weight.shape[2]
    cols = min(BLOCK_COLS, hidden)
    twice_rank = down.shape[-1]
    rows = token_count // CHUNKS
    segs = adapters.shape[1]
    dma = pltpu.SemaphoreType.DMA
    any_space = pl.BlockSpec(memory_space=pl.ANY)
    smem = pl.BlockSpec(memory_space=pltpu.SMEM)
    leaf = up.shape[1:]
    vmem = pltpu.VMEM
    return pl.pallas_call(
        fused_kernel,
        out_shape=(
            jax.ShapeDtypeStruct((n, token_count, depth), tokens.dtype),
            jax.ShapeDtypeStruct((token_count, hidden), jnp.bfloat16),
        ),
        in_specs=[smem] * 3 + [any_space] * 4,
        out_specs=(any_space,) * 2,
        scratch_shapes=[
            vmem((2, token_count, hidden), jnp.float32),
            vmem((2, token_count, depth), tokens.dtype),
            vmem((2, 2, depth, 2, cols), weight.dtype),
            vmem((n, depth, twice_rank), down.dtype),
            vmem((token_count, twice_rank), jnp.float32),
            vmem((n,) + leaf, up.dtype),
            vmem((groups, segs) + leaf, up.dtype),
            vmem((groups, segs) + leaf, up.dtype),
            vmem((size,) + leaf, up.dtype),
            vmem((CHUNKS, n, rows // n, twice_rank), jnp.bfloat16),
            vmem((CHUNKS, n, rows // n, twice_rank), jnp.bfloat16),
            vmem((CHUNKS, n, rows // n, twice_rank), jnp.bfloat16),
            vmem((2, rows, hidden), jnp.bfloat16),
            dma((n, CHUNKS)),
            dma((n, CHUNKS)),
            dma((n, CHUNKS)),
            dma((n, CHUNKS)),
            dma((3,)),
            dma((2, 2)),
            dma((2, groups)),
            dma((2, n)),
            dma((2, groups)),
            dma((2, size)),
            dma((2, CHUNKS, n)),
            dma((2, CHUNKS, n)),
            dma((6,)),
        ],
        compiler_params=pltpu.CompilerParams(
            vmem_limit_bytes=VMEM_LIMIT, has_side_effects=True
        ),
        name="fused",
    )(counts, adapters, pool_rows, tokens, weight, down, up)


def compute_fused(
    tokens,
    gate_up_weight,
    down_factor_pool,
    up_factor_pool,
    segment_adapters,
    segment_tile_counts,
    adapter_pool_rows,
):
    groups = lax.axis_size("grp")
    size, cores = lax.axis_size("tp"), lax.axis_size("cores")
    depth = tokens.shape[1]
    down = down_factor_pool.reshape(size * cores // groups, depth, down_factor_pool.shape[2])
    up = up_factor_pool.reshape(up_factor_pool.shape[2:])
    return fused_call(
        segment_tile_counts,
        segment_adapters,
        adapter_pool_rows,
        tokens,
        gate_up_weight,
        down,
        up,
        groups,
        size,
        cores,
    )[1]


def fits(mesh):
    size, cores, groups = mesh.shape["tp"], mesh.shape["cores"], mesh.shape["grp"]
    return cores == 2 and size == 4 and size * cores % groups == 0


def per_device(*args):
    return compute(*args)


def compute(
    tokens,
    gate_up_weight,
    down_factor_pool,
    up_factor_pool,
    segment_adapters,
    segment_tile_counts,
    adapter_pool_rows,
):
    groups = lax.axis_size("grp")
    tp_size, cores_size = lax.axis_size("tp"), lax.axis_size("cores")
    n = tp_size * cores_size
    token_count, depth = tokens.shape
    local_hidden_width = gate_up_weight.shape[2]
    twice_rank = down_factor_pool.shape[2]
    narrow = local_hidden_width // groups
    seg_count = segment_adapters.shape[1]
    half = token_count // 2

    me = ring_position(lax.axis_index("tp"), lax.axis_index("cores"), tp_size)
    order = [ring_device(k, tp_size, cores_size) for k in range(n)]
    forward = [(order[k], order[(k + 1) % n]) for k in range(n)]
    backward = [(order[(k + 1) % n], order[k]) for k in range(n)]

    def owner(shift):
        return ring_device((me + shift + n) % n, tp_size, cores_size).astype(jnp.int32)

    full_steps = (n - 1) // 2
    lefts, rights = [tokens], [tokens]
    for _ in range(1, full_steps + 1):
        lefts.append(lax.ppermute(lefts[-1], TP, forward))
        rights.append(lax.ppermute(rights[-1], TP, backward))
    last_top = lax.ppermute(lefts[-1][:half], TP, forward)
    last_bottom = lax.ppermute(rights[-1][half:], TP, backward)

    piece = depth // groups
    a = down_factor_pool.reshape(n // groups, groups, piece, twice_rank)
    a = lax.all_to_all(a, "grp", split_axis=1, concat_axis=0, tiled=True)
    a = a.reshape(n, piece, twice_rank)
    a = lax.all_to_all(a, TP, split_axis=0, concat_axis=0, tiled=True)
    b = up_factor_pool.reshape(up_factor_pool.shape[2:])
    b = lax.all_to_all(b, TP, split_axis=0, concat_axis=0, tiled=True)
    slots = jnp.take(adapter_pool_rows, segment_adapters, mode="clip")
    a = group_exchange(a, slots)
    b = group_exchange(b, slots)
    block_cols = narrow
    if narrow % 128:
        block_cols = local_hidden_width
        b = b.reshape(groups, seg_count, b.shape[2], 2, narrow)
        b = jnp.transpose(b, (1, 2, 3, 0, 4))
        b = b.reshape(1, seg_count, b.shape[1], 2 * block_cols)

    tile_count = token_count // TILE
    tile_seg = tile_segments(segment_tile_counts[0], tile_count).astype(jnp.int32)
    row_seg = jnp.repeat(tile_seg, TILE)[:, None]
    partial = None
    for j in range(seg_count):
        term = jnp.dot(
            tokens, a[:, j].reshape(depth, twice_rank), preferred_element_type=jnp.float32
        )
        partial = term if partial is None else jnp.where(row_seg == j, term, partial)
    share = token_count // n
    partial = lax.all_to_all(
        partial.reshape(n, share, twice_rank), TP, split_axis=0, concat_axis=0, tiled=True
    )
    own = jnp.sum(partial, axis=0).astype(jnp.bfloat16)
    shrunk = lax.all_to_all(
        jnp.broadcast_to(own[None], (n, share, twice_rank)),
        TP,
        split_axis=0,
        concat_axis=0,
        tiled=True,
    ).reshape(token_count, twice_rank)

    acc = None
    for s in range(1, full_steps + 1):
        xs = [lefts[s], rights[s]]
        rows = [owner(-s), owner(s)]
        if s == 1:
            xs.insert(0, tokens)
            rows.insert(0, owner(0))
        acc = partial_matmul(xs, gate_up_weight, jnp.stack(rows), acc, block_cols)
    return final_matmul(
        last_top, last_bottom, gate_up_weight, jnp.stack([owner(n // 2)]), acc, shrunk, b, tile_seg
    )


def fused(*args):
    return compute_fused(*args)


def solution(mesh):
    direct = fits(mesh)
    return jax.shard_map(
        fused if direct else per_device,
        mesh=mesh,
        in_specs=(
            P("grp", ("tp", "cores")),
            P(None, None, ("tp", "cores")),
            P(("tp", "cores"), "grp", None),
            P(("tp", "cores"), "grp", None, None, None),
            P(),
            P("grp", None),
            P(),
        ),
        out_specs=P("grp", ("tp", "cores")),
        check_vma=False,
    )
```

```python
import functools

import jax
import jax.numpy as jnp
from jax import lax
from jax.experimental import pallas as pl
from jax.experimental.pallas import tpu as pltpu
from jax.sharding import PartitionSpec as P


TILE = 128
VMEM_LIMIT = 60 * 1024 * 1024

adapter_scale = 0.5


TP = ("tp", "cores")


def tile_segments(tile_lengths, tile_count):
    bounds = jnp.cumsum(tile_lengths)
    positions = jnp.arange(tile_count, dtype=jnp.int32)
    return jnp.sum((bounds[None, :] <= positions[:, None]).astype(jnp.int32), axis=1)


def ring_device(position, tp_size, cores_size):
    c = position // tp_size
    t = position % tp_size
    t = t + (c % 2) * (tp_size - 1 - 2 * t)
    return t * cores_size + c


def ring_position(tp_index, cores_index, tp_size):
    t = tp_index + (cores_index % 2) * (tp_size - 1 - 2 * tp_index)
    return cores_index * tp_size + t


def partial_kernel(count, with_acc, rows_ref, *refs):
    xs, ws = refs[:count], refs[count : 2 * count]
    out = refs[-1]
    ws = [jnp.swapaxes(w[...], 0, 1) for w in ws]
    for h in range(2):
        total = refs[2 * count][h] if with_acc else None
        for x, w in zip(xs, ws):
            term = jnp.dot(x[...], w[h], preferred_element_type=jnp.float32)
            total = term if total is None else total + term
        out[h] = total


def partial_matmul(xs, weight, rows, acc, block_cols):
    count = len(xs)
    tokens, depth = xs[0].shape
    hidden = weight.shape[2]
    block_cols = min(block_cols, 256)
    in_specs = [pl.BlockSpec((tokens, depth), lambda j, r: (0, 0))] * count
    for k in range(count):
        in_specs.append(
            pl.BlockSpec((depth, 2, block_cols), lambda j, r, k=k: (r[k], 0, j))
        )
    acc_spec = pl.BlockSpec((2, tokens, block_cols), lambda j, r: (0, 0, j))
    operands = list(xs) + [weight] * count
    aliases = {}
    if acc is not None:
        in_specs.append(acc_spec)
        aliases = {1 + len(operands): 0}
        operands.append(acc)
    return pl.pallas_call(
        functools.partial(partial_kernel, count, acc is not None),
        out_shape=jax.ShapeDtypeStruct((2, tokens, hidden), jnp.float32),
        grid_spec=pltpu.PrefetchScalarGridSpec(
            num_scalar_prefetch=1,
            grid=(hidden // block_cols,),
            in_specs=in_specs,
            out_specs=acc_spec,
        ),
        input_output_aliases=aliases,
        compiler_params=pltpu.CompilerParams(vmem_limit_bytes=VMEM_LIMIT),
        cost_estimate=pl.CostEstimate(
            flops=4 * count * tokens * depth * hidden,
            bytes_accessed=count * 4 * depth * hidden + 16 * tokens * hidden,
            transcendentals=0,
        ),
    )(rows, *operands)


def final_kernel(tiles_per_half, rank, rows_ref, seg_ref, xt, xb, w, acc, shrunk, b, out, total):
    narrow = out.shape[1]
    w = jnp.swapaxes(w[...], 0, 1)
    for p, x in enumerate((xt, xb)):
        for h in range(2):
            span = slice(p * x.shape[0], (p + 1) * x.shape[0])
            total[h, span] = acc[h, span] + jnp.dot(
                x[...], w[h], preferred_element_type=jnp.float32
            )
        for t in range(p * tiles_per_half, (p + 1) * tiles_per_half):
            seg = seg_ref[t]
            span = slice(t * TILE, (t + 1) * TILE)
            both = []
            for h in range(2):
                delta = jnp.dot(
                    shrunk[span, h * rank : (h + 1) * rank],
                    b[0, seg, :, h * narrow : (h + 1) * narrow],
                    preferred_element_type=jnp.float32,
                )
                both.append(total[h, span] + adapter_scale * delta)
            gate, up = both
            out[span] = (gate / (1.0 + jnp.exp(-gate)) * up).astype(out.dtype)


def final_matmul(xt, xb, weight, rows, acc, shrunk, b_chosen, tile_seg):
    half, depth = xt.shape
    tokens = 2 * half
    hidden = weight.shape[2]
    blocks, segs, rank, twice = b_chosen.shape
    narrow = twice // 2
    return pl.pallas_call(
        functools.partial(final_kernel, half // TILE, rank),
        out_shape=jax.ShapeDtypeStruct((tokens, hidden), jnp.bfloat16),
        grid_spec=pltpu.PrefetchScalarGridSpec(
            num_scalar_prefetch=2,
            grid=(blocks,),
            in_specs=[
                pl.BlockSpec((half, depth), lambda j, r, s: (0, 0)),
                pl.BlockSpec((half, depth), lambda j, r, s: (0, 0)),
                pl.BlockSpec((depth, 2, narrow), lambda j, r, s: (r[0], 0, j)),
                pl.BlockSpec((2, tokens, narrow), lambda j, r, s: (0, 0, j)),
                pl.BlockSpec((tokens, 2 * rank), lambda j, r, s: (0, 0)),
                pl.BlockSpec((1, segs, rank, twice), lambda j, r, s: (j, 0, 0, 0)),
            ],
            out_specs=pl.BlockSpec((tokens, narrow), lambda j, r, s: (0, j)),
            scratch_shapes=[pltpu.VMEM((2, tokens, narrow), jnp.float32)],
        ),
        compiler_params=pltpu.CompilerParams(vmem_limit_bytes=VMEM_LIMIT),
        cost_estimate=pl.CostEstimate(
            flops=4 * tokens * (depth + rank) * hidden,
            bytes_accessed=4 * depth * hidden + 10 * tokens * hidden,
            transcendentals=tokens * hidden,
        ),
    )(rows, tile_seg, xt, xb, weight, acc, shrunk, b_chosen)


def group_exchange(pool, slots):
    groups = lax.axis_size("grp")
    g = lax.axis_index("grp")
    parts = []
    for k in range(groups):
        wanted = lax.dynamic_index_in_dim(slots, (g + k) % groups, 0, keepdims=False)
        part = jnp.take(pool, wanted, axis=0, mode="clip")
        if k:
            pairs = [(i, (i + k) % groups) for i in range(groups)]
            part = lax.ppermute(part, "grp", pairs)
        parts.append(part)
    sources = (g + groups - jnp.arange(groups)) % groups
    return jnp.take(jnp.stack(parts), sources, axis=0, mode="clip")


MESH = pl.DeviceIdType.MESH
CHUNKS = 4
END_SHIFT = 0
BLOCK_COLS = 512


def table(rows, i, k):
    total = 0
    for a, row in enumerate(rows):
        for b, value in enumerate(row):
            if value:
                total = total + jnp.where((i == a) & (k == b), value, 0)
    return total


def reach(size):
    return [sorted(range(size), key=lambda t, z=z: (abs(t - z), t)) for z in range(size)]


def shifted(size, source, dest, c):
    to_end = ((dest == 0) | (dest == size - 1)) & (c >= CHUNKS - END_SHIFT)
    from_end = (source == 0) | (source == size - 1)
    return to_end | from_end


def fused_kernel(
    counts,
    adapters,
    pool_rows,
    tokens,
    weight,
    down,
    up,
    xg,
    out,
    acc,
    xv,
    wbuf,
    d_all,
    low,
    u1,
    u_pick,
    u_all,
    u_relay,
    part,
    s_in,
    shrunk,
    stage,
    recv,
    up_sem,
    dn_sem,
    y_sem,
    x_sem,
    w_sem,
    d_sem,
    u1_sem,
    u2_sem,
    ur_sem,
    s_sem,
    g_sem,
    o_sem,
):
    groups = lax.axis_size("grp")
    size, cores = lax.axis_size("tp"), lax.axis_size("cores")
    n = size * cores
    g, z, y = lax.axis_index("grp"), lax.axis_index("tp"), lax.axis_index("cores")
    me = z * cores + y
    other = 1 - y
    token_count, depth = tokens.shape
    rows = token_count // CHUNKS
    hidden = weight.shape[2]
    cols = wbuf.shape[-1]
    blocks = hidden // cols
    per = n // groups
    order = reach(size)
    seg_count = adapters.shape[1]
    rank = up.shape[1]
    narrow = up.shape[2] // 2
    piece_rows = rows // n

    ends = []
    for k in range(seg_count):
        ends.append(counts[0, k] + (ends[-1] if ends else 0))
    tile_seg = []
    for t in range(token_count // TILE):
        seg = 0
        for k in range(seg_count - 1):
            seg = seg + jnp.where(ends[k] <= t, 1, 0)
        tile_seg.append(seg)

    def peer(k):
        return {"grp": lax.rem(g + k, groups)}

    def span(c):
        if isinstance(c, int):
            return pl.ds(c * rows, rows)
        return pl.ds(pl.multiple_of(c * rows, rows), rows)

    def remote(src, dst, send, receive, dev):
        return pltpu.make_async_remote_copy(
            src_ref=src,
            dst_ref=dst,
            send_sem=send,
            recv_sem=receive,
            device_id=dev,
            device_id_type=MESH,
        )


    def hop(src, s, c, sems, dev):
        return remote(src, xg.at[s, span(c)], sems.at[s, c], recv.at[s, c], dev)

    up_dev, dn_dev, y_dev = {"tp": z + 1}, {"tp": z - 1}, {"cores": other}

    def arrived(s, c):
        hop(xg.at[s, span(c)], s, c, y_sem, y_dev).wait_recv()

    def forward(s, c, sems, dev):
        hop(xg.at[s, span(c)], s, c, sems, dev).start()

    def send_row(c):
        src = tokens.at[span(c)]

        @pl.when(z + 1 < size)
        def _():
            hop(src, me, c, up_sem, up_dev).start()

        @pl.when(z >= 1)
        def _():
            hop(src, me, c, dn_sem, dn_dev).start()

    def send_mate(c):
        hop(tokens.at[span(c)], me, c, y_sem, y_dev).start()

    def row_arrival(r, c, first):
        lo, hi = z - r, z + r

        @pl.when(lo >= 0)
        def _():
            s = lo * cores + y
            arrived(s, c)

            @pl.when(z + 1 < size)
            def _():
                forward(s, c, up_sem, up_dev)

            @pl.when(jnp.logical_not(shifted(size, lo, z, c)) if first else z >= 0)
            def _():
                forward(s, c, y_sem, y_dev)

        @pl.when(hi < size)
        def _():
            s = hi * cores + y
            arrived(s, c)

            @pl.when(z >= 1)
            def _():
                forward(s, c, dn_sem, dn_dev)

            @pl.when(jnp.logical_not(shifted(size, hi, z, c)) if first else z >= 0)
            def _():
                forward(s, c, y_sem, y_dev)

    def mate_arrival(c):
        s = z * cores + other
        arrived(s, c)

        @pl.when((z + 1 < size) & shifted(size, z, z + 1, c))
        def _():
            forward(s, c, up_sem, up_dev)

        @pl.when((z >= 1) & shifted(size, z, z - 1, c))
        def _():
            forward(s, c, dn_sem, dn_dev)


    def w_copy(piece, j, slot, k):
        return pltpu.make_async_copy(
            weight.at[
                pl.ds(pl.multiple_of(piece * depth, depth), depth),
                slice(None),
                pl.ds(pl.multiple_of(j * cols, cols), cols),
            ],
            wbuf.at[slot, k],
            w_sem.at[slot, k],
        )

    def first_tiles(pieces):
        for k, piece in enumerate(pieces):
            w_copy(piece, 0, 0, k).start()

    def multiply(pieces, j, low_row, count, first, then):
        slot = lax.rem(j, 2)

        @pl.when(j + 1 == blocks)
        def _():
            first_tiles(then)

        @pl.when(j + 1 < blocks)
        def _():
            for k, piece in enumerate(pieces):
                w_copy(piece, j + 1, 1 - slot, k).start()

        at = pl.ds(pl.multiple_of(j * cols, cols), cols)
        where = pl.ds(low_row, count)
        for k, piece in enumerate(pieces):
            w_copy(piece, j, slot, k).wait()
        ws = [jnp.swapaxes(wbuf[slot, k], 0, 1) for k in range(len(pieces))]
        for h in range(2):
            total = None if first else acc[h, where, at]
            for k in range(len(pieces)):
                term = jnp.dot(xv[k, where], ws[k][h], preferred_element_type=jnp.float32)
                total = term if total is None else total + term
            acc[h, where, at] = total

    def run_round(pieces, sources, then, first=False, project=True, hooks=(), start=0, count=None):
        count = token_count if count is None else count
        at = pl.ds(start, count)
        copies = [
            pltpu.make_async_copy(src.at[at], xv.at[k, at], x_sem.at[k])
            for k, src in enumerate(sources)
        ]
        for copy in copies:
            copy.start()
        for copy in copies:
            copy.wait()
        if project:
            for k, piece in enumerate(pieces):
                low[at] = low[at] + jnp.dot(
                    xv[k, at], d_all[piece], preferred_element_type=jnp.float32
                )
        products(pieces, then, first, hooks, start, count)

    def products(pieces, then, first, hooks, start, count):
        def one(j, carry):
            multiply(pieces, j, start, count, first, then)
            for i, hook in enumerate(hooks):
                if hook is not None:
                    pl.when(j == (i + 1) * blocks // len(hooks) - 1)(hook)
            return carry

        lax.fori_loop(0, blocks, one, 0)


    near_end = (z == 1) | (z == size - 2)
    end = jnp.where(z == 1, 0, size - 1)

    def relayed(p_z, p_y, s_z, s_y):
        return ((p_z == 0) | (p_z == size - 1)) & (p_y != s_y) & (p_z != s_z)

    def relay_dev(p_z, p_y):
        return {"tp": jnp.where(p_z == 0, 1, size - 2), "cores": p_y}

    def scatter(source, final, relay, sems, relay_sems, act):
        for k in range(1, n):
            p = lax.rem(me + k, n)
            p_z, p_y = p // cores, lax.rem(p, cores)
            far = relayed(p_z, p_y, z, y)

            @pl.when(far)
            def _():
                copy = remote(
                    source(p), relay.at[z], sems.at[0, p], relay_sems.at[0, z],
                    relay_dev(p_z, p_y),
                )
                act(copy)

            @pl.when(jnp.logical_not(far))
            def _():
                copy = remote(
                    source(p), final.at[me], sems.at[0, p], sems.at[1, me],
                    {"tp": p_z, "cores": p_y},
                )
                act(copy)

    def relay_copy(final, relay, sems, relay_sems, k):
        s_z = lax.rem(end + k, size)
        s = s_z * cores + other
        return s_z, remote(
            relay.at[s_z], final.at[s], relay_sems.at[1, s_z], sems.at[1, s], {"tp": end}
        )

    def pass_on(final, relay, sems, relay_sems):
        @pl.when(near_end)
        def _():
            for k in range(1, size):
                s_z, copy = relay_copy(final, relay, sems, relay_sems, k)
                remote(
                    relay.at[s_z], relay.at[s_z], relay_sems.at[1, s_z], relay_sems.at[0, s_z],
                    {"tp": end},
                ).wait_recv()
                copy.start()

    def scattered(final, sems):
        for k in range(1, n):
            s = lax.rem(me + k, n)
            remote(final.at[s], final.at[s], sems.at[0, s], sems.at[1, s], y_dev).wait_recv()

    def relays_done(final, relay, sems, relay_sems):
        @pl.when(near_end)
        def _():
            for k in range(1, size):
                relay_copy(final, relay, sems, relay_sems, k)[1].wait_send()

    def started(copy):
        copy.start()

    def sent(copy):
        copy.wait_send()

    def u_source(p):
        return up.at[p]

    def u_scatter(act):
        scatter(u_source, u1, u_relay, u1_sem, ur_sem, act)

    def d_copy(k):
        mine = d_all.at[pl.ds(g * per, per)]
        return remote(down, mine, d_sem.at[0, k], d_sem.at[1, k], peer(k))

    def u2_copy(k):
        return remote(u_pick.at[k], u_all.at[g], u2_sem.at[0, k], u2_sem.at[1, k], peer(k))

    def pick(source, picked, mine):
        for k in range(groups):
            which = lax.rem(g + k, groups)
            for j in range(seg_count):
                value = source[pool_rows[adapters[which, j]]]
                if k:
                    picked[k, j] = value
                else:
                    mine[g, j] = value


    tile_rows = [pool_rows[adapters[g, seg]] for seg in tile_seg]

    def low_send(c):
        base = c * rows
        for t in range(rows // TILE):
            tile = c * (rows // TILE) + t
            value = low[base + t * TILE : base + (t + 1) * TILE]
            value = jnp.where(tile_rows[tile] == me, value, 0.0).astype(part.dtype)
            count = TILE // piece_rows
            for i in range(count):
                part[c, t * count + i] = value[i * piece_rows : (i + 1) * piece_rows]
        for k in range(1, n):
            s_copy(c, k).start()

    def mate(k):
        p = lax.rem(me + k, n)
        return p, {"tp": p // cores, "cores": lax.rem(p, cores)}

    def s_copy(c, k):
        p, dev = mate(k)
        return remote(
            part.at[c, p], s_in.at[c, k], s_sem.at[0, c, k], s_sem.at[1, c, k], dev
        )

    def g_copy(c, k):
        _, dev = mate(k)
        mine = shrunk.at[c, me]
        return remote(mine, mine, g_sem.at[0, c, k], g_sem.at[1, c, k], dev)

    def low_sum(c):
        total = part[c, me].astype(jnp.float32)
        for k in range(1, n):
            s_copy(c, k).wait_recv()
            total = total + s_in[c, k].astype(jnp.float32)
        shrunk[c, me] = total.astype(shrunk.dtype)

    def low_share(c):
        for k in range(1, n):
            g_copy(c, k).start()

    def low_ready(c):
        for k in range(1, n):
            p = lax.rem(me + n - k, n)
            mine = shrunk.at[c, p]
            remote(mine, mine, g_sem.at[0, c, k], g_sem.at[1, c, k], y_dev).wait_recv()

    def here(src, dst, k):
        return pltpu.make_async_copy(src, dst, o_sem.at[k])

    def stage_copy(c):
        return pltpu.make_async_copy(stage.at[c % 2], out.at[span(c)], o_sem.at[4 + c % 2])

    def epilogue(c):
        base = c * rows
        if c >= 2:
            stage_copy(c - 2).wait()

        def one(j, carry):
            at = pl.ds(pl.multiple_of(j * cols, cols), cols)
            m = (j * cols) // narrow
            offset = lax.rem(j * cols, narrow)
            for t in range(rows // TILE):
                tile = c * (rows // TILE) + t
                count = TILE // piece_rows
                x = shrunk[c, t * count : (t + 1) * count].reshape(TILE, 2 * rank)
                both = []
                for h in range(2):
                    delta = jnp.dot(
                        x[:, h * rank : (h + 1) * rank],
                        u_all[
                            m,
                            tile_seg[tile],
                            :,
                            pl.ds(pl.multiple_of(h * narrow + offset, cols), cols),
                        ],
                        preferred_element_type=jnp.float32,
                    )
                    total = acc[h, base + t * TILE : base + (t + 1) * TILE, at]
                    both.append(total + adapter_scale * delta)
                gate, lift = both
                value = gate / (1.0 + jnp.exp(-gate)) * lift
                stage[c % 2, t * TILE : (t + 1) * TILE, at] = value.astype(stage.dtype)
            return carry

        lax.fori_loop(0, blocks, one, 0)
        stage_copy(c).start()

    def drain(i, carry):
        t, c = i // CHUNKS, lax.rem(i, CHUNKS)
        s, across = t * cores + y, t * cores + other

        def done(s, sems, dev):
            hop(xg.at[s, span(c)], s, c, sems, dev).wait_send()

        @pl.when((z + 1 < size) & (t <= z))
        def _():
            done(s, up_sem, up_dev)

        @pl.when((z >= 1) & (t >= z))
        def _():
            done(s, dn_sem, dn_dev)

        near = (t == z - 1) | (t == z + 1)

        @pl.when(jnp.logical_not(near & shifted(size, t, z, c)))
        def _():
            done(s, y_sem, y_dev)

        @pl.when((t == z) & (z + 1 < size) & shifted(size, z, z + 1, c))
        def _():
            done(across, up_sem, up_dev)

        @pl.when((t == z) & (z >= 1) & shifted(size, z, z - 1, c))
        def _():
            done(across, dn_sem, dn_dev)

        return carry

    def all_sent():
        for k in range(1, groups):
            d_copy(k).wait_send()
            u2_copy(k).wait_send()
        u_scatter(sent)
        relays_done(u1, u_relay, u1_sem, ur_sem)
        lax.fori_loop(0, size * CHUNKS, drain, 0)

    def row_piece(i):
        return table(order, z, i) * cores + y

    def cross_piece(i):
        return table(order, z, i) * cores + other

    def near_arrivals(c):
        row_arrival(1, c, True)
        mate_arrival(c)

    def cross_ready(piece):
        for c in range(CHUNKS):
            arrived(piece, c)

    far = cross_piece(size - 1)


    for c in range(CHUNKS):
        send_row(c)
        send_mate(c)
    for k in range(1, groups):
        d_copy(k).start()
    here(down, d_all.at[pl.ds(g * per, per)], 0).start()
    here(up.at[me], u1.at[me], 1).start()
    u_scatter(started)
    first_tiles([me])
    pair = [row_piece(1), cross_piece(0)]
    run_round(
        [me], [tokens], pair, True, False,
        [functools.partial(near_arrivals, c) for c in range(CHUNKS)],
    )
    here(down, d_all.at[pl.ds(g * per, per)], 0).wait()
    for k in range(1, groups):
        d_copy(k).wait_recv()
    low[...] = jnp.dot(xv[0], d_all[me], preferred_element_type=jnp.float32)
    run_round(
        pair, [xg.at[q] for q in pair], [cross_piece(1)],
        hooks=[None, None, functools.partial(pass_on, u1, u_relay, u1_sem, ur_sem), None],
    )
    row_arrival(2, 0, False)
    cross_ready(cross_piece(1))
    run_round(
        [cross_piece(1)], [xg.at[cross_piece(1)]], [row_piece(2)],
        hooks=[functools.partial(row_arrival, 2, c, False) for c in range(1, CHUNKS - 1)],
    )
    row_arrival(2, CHUNKS - 1, False)
    near = row_piece(size - 1)
    run_round(
        [row_piece(2)], [xg.at[row_piece(2)]], [cross_piece(2)],
        hooks=[functools.partial(row_arrival, 3, 0, False)],
    )
    here(up.at[me], u1.at[me], 1).wait()
    scattered(u1, u1_sem)
    pick(u1, u_pick, u_all)
    for k in range(1, groups):
        u2_copy(k).start()
    cross_ready(cross_piece(2))
    run_round(
        [cross_piece(2)], [xg.at[cross_piece(2)]], [near],
        hooks=[None, None, functools.partial(row_arrival, 3, 1, False), None],
    )
    top = token_count // 2
    run_round(
        [near], [xg.at[near]], [far], start=0, count=top,
        hooks=[functools.partial(row_arrival, 3, 2, False)],
    )


    def low_far(c):
        at = pl.ds(c * rows, rows)
        arrived(far, c)
        copy = pltpu.make_async_copy(xg.at[far, span(c)], xv.at[0, at], x_sem.at[0])
        copy.start()
        copy.wait()
        term = jnp.dot(xv[0, at], d_all[far], preferred_element_type=jnp.float32)
        low[at] = low[at] + term
        low_send(c)

    low_far(0)
    low_far(1)
    products(
        [far], [near], False, [functools.partial(row_arrival, 3, 3, False), None], 0, top
    )
    run_round([near], [xg.at[near]], [far], start=top, count=top)
    low_far(2)
    low_sum(0)
    low_sum(1)
    for k in range(1, groups):
        u2_copy(k).wait_recv()
    low_share(0)
    low_share(1)
    low_far(3)
    products([far], [], False, (), top, top)
    for c in range(2, CHUNKS):
        low_sum(c)
    low_ready(0)
    low_share(2)
    low_share(3)
    epilogue(0)
    low_ready(1)
    epilogue(1)
    all_sent()
    low_ready(2)
    epilogue(2)
    low_ready(3)
    epilogue(3)
    for c in range(CHUNKS):
        for k in range(1, n):
            s_copy(c, k).wait_send()
            g_copy(c, k).wait_send()
    for c in range(CHUNKS - 2, CHUNKS):
        stage_copy(c).wait()


def fused_call(counts, adapters, pool_rows, tokens, weight, down, up, groups, size, cores):
    n = size * cores
    token_count, depth = tokens.shape
    hidden = weight.shape[2]
    cols = min(BLOCK_COLS, hidden)
    twice_rank = down.shape[-1]
    rows = token_count // CHUNKS
    segs = adapters.shape[1]
    dma = pltpu.SemaphoreType.DMA
    any_space = pl.BlockSpec(memory_space=pl.ANY)
    smem = pl.BlockSpec(memory_space=pltpu.SMEM)
    leaf = up.shape[1:]
    vmem = pltpu.VMEM
    return pl.pallas_call(
        fused_kernel,
        out_shape=(
            jax.ShapeDtypeStruct((n, token_count, depth), tokens.dtype),
            jax.ShapeDtypeStruct((token_count, hidden), jnp.bfloat16),
        ),
        in_specs=[smem] * 3 + [any_space] * 4,
        out_specs=(any_space,) * 2,
        scratch_shapes=[
            vmem((2, token_count, hidden), jnp.float32),
            vmem((2, token_count, depth), tokens.dtype),
            vmem((2, 2, depth, 2, cols), weight.dtype),
            vmem((n, depth, twice_rank), down.dtype),
            vmem((token_count, twice_rank), jnp.float32),
            vmem((n,) + leaf, up.dtype),
            vmem((groups, segs) + leaf, up.dtype),
            vmem((groups, segs) + leaf, up.dtype),
            vmem((size,) + leaf, up.dtype),
            vmem((CHUNKS, n, rows // n, twice_rank), jnp.bfloat16),
            vmem((CHUNKS, n, rows // n, twice_rank), jnp.bfloat16),
            vmem((CHUNKS, n, rows // n, twice_rank), jnp.bfloat16),
            vmem((2, rows, hidden), jnp.bfloat16),
            dma((n, CHUNKS)),
            dma((n, CHUNKS)),
            dma((n, CHUNKS)),
            dma((n, CHUNKS)),
            dma((3,)),
            dma((2, 2)),
            dma((2, groups)),
            dma((2, n)),
            dma((2, groups)),
            dma((2, size)),
            dma((2, CHUNKS, n)),
            dma((2, CHUNKS, n)),
            dma((6,)),
        ],
        compiler_params=pltpu.CompilerParams(
            vmem_limit_bytes=VMEM_LIMIT, has_side_effects=True
        ),
        name="fused",
    )(counts, adapters, pool_rows, tokens, weight, down, up)


def compute_fused(
    tokens,
    gate_up_weight,
    down_factor_pool,
    up_factor_pool,
    segment_adapters,
    segment_tile_counts,
    adapter_pool_rows,
):
    groups = lax.axis_size("grp")
    size, cores = lax.axis_size("tp"), lax.axis_size("cores")
    depth = tokens.shape[1]
    down = down_factor_pool.reshape(size * cores // groups, depth, down_factor_pool.shape[2])
    up = up_factor_pool.reshape(up_factor_pool.shape[2:])
    return fused_call(
        segment_tile_counts,
        segment_adapters,
        adapter_pool_rows,
        tokens,
        gate_up_weight,
        down,
        up,
        groups,
        size,
        cores,
    )[1]


def fits(mesh):
    size, cores, groups = mesh.shape["tp"], mesh.shape["cores"], mesh.shape["grp"]
    return cores == 2 and size == 4 and size * cores % groups == 0


def per_device(*args):
    return compute(*args)


def compute(
    tokens,
    gate_up_weight,
    down_factor_pool,
    up_factor_pool,
    segment_adapters,
    segment_tile_counts,
    adapter_pool_rows,
):
    groups = lax.axis_size("grp")
    tp_size, cores_size = lax.axis_size("tp"), lax.axis_size("cores")
    n = tp_size * cores_size
    token_count, depth = tokens.shape
    local_hidden_width = gate_up_weight.shape[2]
    twice_rank = down_factor_pool.shape[2]
    narrow = local_hidden_width // groups
    seg_count = segment_adapters.shape[1]
    half = token_count // 2

    me = ring_position(lax.axis_index("tp"), lax.axis_index("cores"), tp_size)
    order = [ring_device(k, tp_size, cores_size) for k in range(n)]
    forward = [(order[k], order[(k + 1) % n]) for k in range(n)]
    backward = [(order[(k + 1) % n], order[k]) for k in range(n)]

    def owner(shift):
        return ring_device((me + shift + n) % n, tp_size, cores_size).astype(jnp.int32)

    full_steps = (n - 1) // 2
    lefts, rights = [tokens], [tokens]
    for _ in range(1, full_steps + 1):
        lefts.append(lax.ppermute(lefts[-1], TP, forward))
        rights.append(lax.ppermute(rights[-1], TP, backward))
    last_top = lax.ppermute(lefts[-1][:half], TP, forward)
    last_bottom = lax.ppermute(rights[-1][half:], TP, backward)

    piece = depth // groups
    a = down_factor_pool.reshape(n // groups, groups, piece, twice_rank)
    a = lax.all_to_all(a, "grp", split_axis=1, concat_axis=0, tiled=True)
    a = a.reshape(n, piece, twice_rank)
    a = lax.all_to_all(a, TP, split_axis=0, concat_axis=0, tiled=True)
    b = up_factor_pool.reshape(up_factor_pool.shape[2:])
    b = lax.all_to_all(b, TP, split_axis=0, concat_axis=0, tiled=True)
    slots = jnp.take(adapter_pool_rows, segment_adapters, mode="clip")
    a = group_exchange(a, slots)
    b = group_exchange(b, slots)
    block_cols = narrow
    if narrow % 128:
        block_cols = local_hidden_width
        b = b.reshape(groups, seg_count, b.shape[2], 2, narrow)
        b = jnp.transpose(b, (1, 2, 3, 0, 4))
        b = b.reshape(1, seg_count, b.shape[1], 2 * block_cols)

    tile_count = token_count // TILE
    tile_seg = tile_segments(segment_tile_counts[0], tile_count).astype(jnp.int32)
    row_seg = jnp.repeat(tile_seg, TILE)[:, None]
    partial = None
    for j in range(seg_count):
        term = jnp.dot(
            tokens, a[:, j].reshape(depth, twice_rank), preferred_element_type=jnp.float32
        )
        partial = term if partial is None else jnp.where(row_seg == j, term, partial)
    share = token_count // n
    partial = lax.all_to_all(
        partial.reshape(n, share, twice_rank), TP, split_axis=0, concat_axis=0, tiled=True
    )
    own = jnp.sum(partial, axis=0).astype(jnp.bfloat16)
    shrunk = lax.all_to_all(
        jnp.broadcast_to(own[None], (n, share, twice_rank)),
        TP,
        split_axis=0,
        concat_axis=0,
        tiled=True,
    ).reshape(token_count, twice_rank)

    acc = None
    for s in range(1, full_steps + 1):
        xs = [lefts[s], rights[s]]
        rows = [owner(-s), owner(s)]
        if s == 1:
            xs.insert(0, tokens)
            rows.insert(0, owner(0))
        acc = partial_matmul(xs, gate_up_weight, jnp.stack(rows), acc, block_cols)
    return final_matmul(
        last_top, last_bottom, gate_up_weight, jnp.stack([owner(n // 2)]), acc, shrunk, b, tile_seg
    )


def fused(*args):
    return compute_fused(*args)


def solution(mesh):
    direct = fits(mesh)
    return jax.shard_map(
        fused if direct else per_device,
        mesh=mesh,
        in_specs=(
            P("grp", ("tp", "cores")),
            P(None, None, ("tp", "cores")),
            P(("tp", "cores"), "grp", None),
            P(("tp", "cores"), "grp", None, None, None),
            P(),
            P("grp", None),
            P(),
        ),
        out_specs=P("grp", ("tp", "cores")),
        check_vma=False,
    )
```
